256 devices in a mesh: dp: 8 (over x, core), ctx: 32 (over z, y).
Axes of the slice: x: 4, y: 4, z: 8, core: 2. Of those that a mesh axis runs over, the one named last changes fastest.
Arguments:
- queries: bfloat16 [8, 64, 24576], P('dp', 'ctx'), may hold values from -6 to 6
- grad_out: bfloat16 [8, 64, 16384], P('dp', 'ctx'), may hold values from -64 to 64
- latent: bfloat16 [8, 4096, 576], P('dp', 'ctx'), may hold values from -6 to 6
- latent_up: bfloat16 [512, 32768], P(None, 'ctx'), may hold values from -0.25 to 0.25
- query_start: int32 [8], P('dp'), may hold values from 2 to 4032
- key_lengths: int32 [8], P('dp'), may hold values from 66 to 4096, as said below
Outputs:
- grad_queries: float32 [8, 64, 24576], P('dp', 'ctx')
- grad_latent: float32 [8, 4096, 576], P('dp', 'ctx')
- grad_latent_up: float32 [512, 32768], P('dp', 'ctx')
The draws below stay inside these ranges and needn't reach their ends.
Inputs may be any that keep to these rules, and one draw needn't show every extreme that they name: key_lengths[g] is at most query_start[g] + 64.
All inputs are finite; a program needn't handle non-finite values.
Results may differ from the reference program's by a relative error of at most 0.015.
Values may be sent and summed in bfloat16 or wider, within the bound.
No kernel may reach another device: no remote copies, remote signals or barrier semaphores. Data moves between devices by JAX's collectives and lax.ppermute only.
A program may use at most 128 MiB of HBM per device.

```python
import math
import jax
import jax.numpy as jnp
from jax import lax

H = 128
DN = 128
DR = 64
DV = 128
C = 512
Q = 64
L = 4096
GROUPS = 8
N_CTX = 32


def windows(key):
    base_key = jax.random.fold_in(key, 101)
    first_key, second_key, third_key = jax.random.split(base_key, 3)
    starts = jax.random.randint(first_key, (GROUPS,), 2, L - Q + 1)
    lengths = jax.random.randint(second_key, (GROUPS,), Q + 2, starts + Q + 1)
    widest = jax.random.randint(third_key, (), 0, GROUPS)
    picked = jnp.arange(GROUPS) == widest
    starts = jnp.where(picked, L - Q, starts)
    lengths = jnp.where(picked, L, lengths)
    return (starts.astype(jnp.int32), lengths.astype(jnp.int32))


def draw_query_start(key, part):
    return windows(key)[0]


def draw_key_lengths(key, part):
    return windows(key)[1]


def draw_queries(key, part):
    own_key = jax.random.fold_in(key, 202)
    full_shape = (GROUPS, Q, H, DN + DR)
    values = jnp.clip(jax.random.normal(own_key, full_shape, jnp.float32), -6.0, 6.0)
    return values.reshape(GROUPS, Q, H * (DN + DR)).astype(jnp.bfloat16)


def draw_latent(key, part):
    own_key = jax.random.fold_in(key, 303)
    full_shape = (GROUPS, L, C + DR)
    values = jnp.clip(jax.random.normal(own_key, full_shape, jnp.float32), -6.0, 6.0)
    return values.astype(jnp.bfloat16)


def block_scale(key, extent, pieces, smallest, high):
    factor_of, own = 1.0, jax.random.fold_in(key, 6)
    for axis_at, shards_of in pieces:
        heights = jnp.exp(jax.random.uniform(jax.random.fold_in(own, axis_at), (shards_of,), jnp.float32, smallest / len(pieces), high / len(pieces)))
        factor_of = factor_of * jnp.repeat(heights, extent[axis_at] // shards_of).reshape([-1 if axis == axis_at else 1 for axis in range(len(extent))])
    return factor_of


def scatter_about(key, dims, width, reach, pieces=(), kind=jnp.bfloat16):
    gain = block_scale(key, dims, pieces, -0.22, 0.18) if pieces else 1.0
    array = jax.random.normal(key, dims, jnp.float32) * width * gain
    return jnp.minimum(jnp.maximum(array, -reach), reach).astype(kind)


def setup_inputs(seed: int = 0) -> dict:
    streams_of = jax.random.split(jax.random.key(seed), 7)
    queries = draw_queries(jax.random.fold_in(streams_of[6], 71), 0)
    grad_out = jnp.clip(jax.random.uniform(streams_of[1], (GROUPS, Q, H * DV), jnp.float32, -64.0, 64.0) * block_scale(streams_of[1], (GROUPS, Q, H * DV), ((0, 8), (1, 32)), -0.4, 0.0), -64.0, 64.0).astype(jnp.bfloat16)
    latent = draw_latent(jax.random.fold_in(streams_of[6], 71), 0)
    latent_up = scatter_about(streams_of[3], (C, H * (DN + DV)), C ** -0.5, 0.25, ((1, 32),))
    query_start = draw_query_start(jax.random.fold_in(streams_of[6], 71), 0)
    key_lengths = draw_key_lengths(jax.random.fold_in(streams_of[6], 71), 0)
    return {"queries": queries, "grad_out": grad_out, "latent": latent, "latent_up": latent_up, "query_start": query_start, "key_lengths": key_lengths}


MSCALE = 0.1 * math.log(40.0) + 1.0
NEG_FILL = -1e+30

def lowered(values):
    return lax.optimization_barrier(values.astype(jnp.bfloat16)).astype(jnp.float32)

def head_group(q_part, g_part, w_part, all_keys, visible, score_scale):
    q_nope = q_part[:, :, :DN]
    q_rope = q_part[:, :, DN:]
    w_key = w_part[:, :, :DN].astype(jnp.float32)
    w_value = w_part[:, :, DN:].astype(jnp.float32)
    q_latent = lowered(jnp.einsum('qhd,chd->qhc', q_nope.astype(jnp.float32), w_key))
    g_latent = lowered(jnp.einsum('qhd,chd->qhc', g_part.astype(jnp.float32), w_value))
    q_full = jnp.concatenate([q_latent, q_rope.astype(jnp.float32)], axis=2)
    key_float = all_keys.astype(jnp.float32)
    raw = score_scale * jnp.einsum('qhc,kc->qhk', q_full, key_float)
    seen = visible[:, None, :]
    masked = jnp.where(seen, raw, NEG_FILL)
    row_peak = lax.optimization_barrier(jnp.max(masked, axis=2, keepdims=True))
    weights = jnp.where(seen, jnp.exp(masked - row_peak), 0.0)
    attn = weights / lax.optimization_barrier(jnp.sum(weights, axis=2, keepdims=True))
    attn_low = lowered(attn)
    o_latent = jnp.einsum('qhk,kc->qhc', attn_low, key_float[:, :C])
    grad_probs = jnp.einsum('qhc,kc->qhk', g_latent, key_float[:, :C])
    row_dot = lax.optimization_barrier(jnp.sum(attn_low * grad_probs, axis=2, keepdims=True))
    grad_scores = lowered(score_scale * attn * (grad_probs - row_dot))
    query_grad = jnp.einsum('qhk,kc->qhc', grad_scores, key_float)
    key_side = jnp.einsum('qhk,qhc->kc', grad_scores, q_full)
    value_side = jnp.einsum('qhk,qhc->kc', attn_low, g_latent)
    key_term = lowered(key_side + jnp.pad(value_side, ((0, 0), (0, DR))))
    grad_lat = lowered(query_grad[:, :, :C])
    grad_nope = jnp.einsum('qhc,chd->qhd', grad_lat, w_key)
    grad_query = jnp.concatenate([grad_nope, query_grad[:, :, C:]], axis=2)
    key_weight = jnp.einsum('qhc,qhd->chd', grad_lat, q_nope.astype(jnp.float32))
    value_weight = jnp.einsum('qhc,qhd->chd', lowered(o_latent), g_part.astype(jnp.float32))
    return (grad_query, key_term, jnp.concatenate([key_weight, value_weight], axis=2))

def reference(queries, grad_out, latent, latent_up, query_start, key_lengths):
    score_scale = MSCALE * MSCALE / math.sqrt(DN + DR)
    heads_dev = H // N_CTX
    weight_parts = latent_up.reshape(C, N_CTX, heads_dev, DN + DV).transpose(1, 0, 2, 3)
    key_pos = jnp.arange(L, dtype=jnp.int32)
    query_off = jnp.arange(Q, dtype=jnp.int32)

    def one_group(weight_total, inputs):
        q_group, g_group, key_group, slice_start, key_len = inputs
        window_low = slice_start + Q - key_len
        visible = (key_pos[None, :] >= window_low) & (key_pos[None, :] <= slice_start + query_off[:, None])
        q_parts = q_group.reshape(Q, N_CTX, heads_dev, DN + DR).transpose(1, 0, 2, 3)
        g_parts = g_group.reshape(Q, N_CTX, heads_dev, DV).transpose(1, 0, 2, 3)

        def one_part(key_total, part):
            q_part, g_part, w_part = part
            grad_query, key_term, weight_term = head_group(q_part, g_part, w_part, key_group, visible, score_scale)
            return (key_total + key_term, (grad_query, weight_term))
        key_total, (query_grads, weight_terms) = lax.scan(one_part, jnp.zeros((L, C + DR), jnp.float32), (q_parts, g_parts, weight_parts))
        grad_rows = query_grads.transpose(1, 0, 2, 3).reshape(Q, H * (DN + DR))
        weight_sum = weight_terms.transpose(1, 0, 2, 3).reshape(C, H * (DN + DV))
        return (weight_total + weight_sum, (grad_rows, key_total))
    weight_total, (grad_queries, grad_latent) = lax.scan(one_group, jnp.zeros((C, H * (DN + DV)), jnp.float32), (queries, grad_out, latent, query_start, key_lengths))
    return (grad_queries, grad_latent, weight_total)
```

```python
import math

import jax
import jax.numpy as jnp
from jax import lax
from jax.sharding import Mesh
from jax.sharding import PartitionSpec as P

DN = 128
DR = 64
DV = 128
C = 512
W = C + DR
NZ = 8
NY = 4
DP = ("x", "core")
CTX = ("z", "y")
MSCALE = 0.1 * math.log(40.0) + 1.0
SCALE = MSCALE * MSCALE / math.sqrt(DN + DR)
NEG_FILL = -1e30
BF = jnp.bfloat16
F32 = jnp.float32


def swap_pairs():
    pairs = []
    for c in range(2):
        for y in range(NY):
            home = (y >> 1) == c
            pairs.append((c * NY + y, c * NY + y if home else (1 - c) * NY + 3 - y))
    return pairs


def swap(v):
    return lax.ppermute(v, ("core", "y"), swap_pairs())


def other_core(v):
    return lax.ppermute(v, "core", [(0, 1), (1, 0)])


def pair_y(v):
    return lax.ppermute(v, "y", [(i, i ^ 1) for i in range(NY)])


def along_z(v, step):
    return lax.ppermute(v, "z", [(i, (i + step) % NZ) for i in range(NZ)])


def dot(a, b, da, db):
    return lax.dot_general(a, b, (((da,), (db,)), ((), ())), preferred_element_type=F32)


def local(queries, grad_out, latent, latent_up, query_start, key_lengths):
    heads = latent_up.shape[1] // (DN + DV)
    own_q = queries.shape[1]
    ndev = NZ * NY
    nq = own_q * ndev
    rows = nq * heads
    blk = latent.shape[1]

    ints = jnp.concatenate([query_start, key_lengths])
    ints = swap(ints)
    start, length = ints[0], ints[1]
    keys = swap(latent[0])

    both = jnp.concatenate(
        [
            queries.reshape(own_q, ndev, heads * (DN + DR)),
            grad_out.reshape(own_q, ndev, heads * DV),
        ],
        axis=2,
    )
    both = jnp.moveaxis(both, 1, 0)
    both = lax.all_to_all(both, CTX, 0, 0, tiled=True).reshape(nq, heads * (DN + DR + DV))
    query_all = both[:, : heads * (DN + DR)].reshape(nq, heads, DN + DR)
    grad_heads = both[:, heads * (DN + DR) :].reshape(nq, heads, DV)
    weights_all = latent_up.reshape(C, heads, DN + DV)
    q_nope = query_all[:, :, :DN]
    q_rope = query_all[:, :, DN:]
    w_key = weights_all[:, :, :DN]
    w_value = weights_all[:, :, DN:]
    q_latent = jnp.einsum("qhd,chd->qhc", q_nope, w_key, preferred_element_type=F32).astype(BF)
    g_latent = jnp.einsum("qhd,chd->qhc", grad_heads, w_value, preferred_element_type=F32).astype(
        BF
    )
    qg = jnp.concatenate([q_latent, q_rope, g_latent], axis=2).reshape(rows, W + C)
    qg = swap(qg)
    qg = jnp.concatenate([qg, other_core(qg)], axis=0)
    q_full = qg[:, :W]
    g_rows = qg[:, W:]

    pair = jnp.concatenate([keys, pair_y(keys)], axis=0)
    pieces = {0: pair}
    f = b = pair
    for j in (1, 2, 3):
        f = along_z(f, 1)
        b = along_z(b, -1)
        pieces[-j] = f
        pieces[j] = b
    half = blk
    pieces[4] = jnp.concatenate([along_z(f[:half], 1), along_z(b[half:], -1)], axis=0)
    offsets = (0, -1, 1, -2, 2, -3, 3, 4)
    all_keys = jnp.concatenate([pieces[d] for d in offsets], axis=0)

    zi = lax.axis_index("z")
    yi = lax.axis_index("y")
    ci = lax.axis_index("core")
    y_own = jnp.where((yi >> 1) == ci, yi, 3 - yi)
    within = jnp.arange(blk, dtype=jnp.int32)
    pair_pos = jnp.concatenate([y_own * blk + within, (y_own ^ 1) * blk + within])
    key_pos = jnp.concatenate([((zi + d) % NZ) * (NY * blk) + pair_pos for d in offsets])
    row_pos = start + (jnp.arange(2 * rows, dtype=jnp.int32) % rows) // heads
    low = start + nq - length

    raw = dot(q_full, all_keys, 1, 1) * SCALE
    visible = (key_pos[None, :] >= low) & (key_pos[None, :] <= row_pos[:, None])
    masked = jnp.where(visible, raw, NEG_FILL)
    peak = jnp.max(masked, axis=1)
    e = jnp.where(visible, jnp.exp(masked - peak[:, None]), 0.0)
    gp = dot(g_rows, all_keys[:, :C], 1, 1)
    total = jnp.sum(e, axis=1)
    rdot = jnp.sum(e * gp, axis=1)
    stats = jnp.stack([peak, total, rdot])
    theirs = other_core(stats)
    theirs = jnp.concatenate([theirs[:, rows:], theirs[:, :rows]], axis=1)
    top = jnp.maximum(peak, theirs[0])
    mine_w = jnp.exp(peak - top)
    their_w = jnp.exp(theirs[0] - top)
    denom = total * mine_w + theirs[1] * their_w
    row_dot = (rdot * mine_w + theirs[2] * their_w) / denom
    attn = e * (mine_w / denom)[:, None]
    probs_low = attn.astype(BF)
    grad_scores = (SCALE * attn * (gp - row_dot[:, None])).astype(BF)

    n2 = 2 * blk
    g_pad = jnp.pad(g_rows, ((0, 0), (0, DR)))

    def key_part(k):
        d = slice(k * n2, (k + 1) * n2)
        return dot(grad_scores[:, d], q_full, 0, 0) + dot(probs_low[:, d], g_pad, 0, 0)

    part = {d: key_part(k) for k, d in enumerate(offsets)}
    f = along_z(part[4][:half].astype(BF), 1)
    b = along_z(part[4][half:].astype(BF), -1)
    f = jnp.concatenate([part[3][:half] + f.astype(F32), part[3][half:]], axis=0)
    b = jnp.concatenate([part[-3][:half], part[-3][half:] + b.astype(F32)], axis=0)
    f = along_z(f.astype(BF), 1)
    b = along_z(b.astype(BF), -1)
    for j in (2, 1):
        f = along_z((part[j] + f.astype(F32)).astype(BF), 1)
        b = along_z((part[-j] + b.astype(F32)).astype(BF), -1)
    mine = part[0] + f.astype(F32) + b.astype(F32)
    mine = mine[:half] + pair_y(mine[half:].astype(BF)).astype(F32)
    key_grad = swap(mine.astype(BF)).astype(F32)

    query_grad = dot(grad_scores, all_keys, 1, 0)
    o_latent = dot(probs_low, all_keys[:, :C], 1, 0)
    qo = jnp.concatenate([query_grad, o_latent], axis=1)
    qo = qo[:rows] + other_core(qo[rows:].astype(BF)).astype(F32)
    qo = swap(qo.astype(BF))
    grad_lat = qo[:, :C].reshape(nq, heads, C)
    grad_rope = qo[:, C:W].reshape(nq, heads, DR)
    o_low = qo[:, W:].reshape(nq, heads, C)
    grad_nope = jnp.einsum("qhc,chd->qhd", grad_lat, w_key, preferred_element_type=F32)
    grad_query = jnp.concatenate([grad_nope.astype(BF), grad_rope], axis=2)
    grad_query = grad_query.reshape(ndev, own_q, heads * (DN + DR))
    back = lax.all_to_all(grad_query, CTX, 0, 0, tiled=True)
    grad_queries = jnp.moveaxis(back, 0, 1).reshape(1, own_q, -1).astype(F32)

    key_weight = jnp.einsum("qhc,qhd->chd", grad_lat, q_nope, preferred_element_type=F32)
    value_weight = jnp.einsum("qhc,qhd->chd", o_low, grad_heads, preferred_element_type=F32)
    terms = jnp.concatenate([key_weight, value_weight], axis=2).astype(BF)
    terms = terms.reshape(8, C // 8, heads * (DN + DV))
    arrived = lax.all_to_all(terms, DP, 0, 0, tiled=True)
    grad_weights = arrived.astype(F32).sum(axis=0)
    return (grad_queries, key_grad[None], grad_weights)


def solution(mesh):
    finer = Mesh(mesh.devices.reshape(4, 2, NZ, NY), ("x", "core", "z", "y"))
    in_specs = (
        P(DP, CTX, None),
        P(DP, CTX, None),
        P(DP, CTX, None),
        P(None, CTX),
        P(DP),
        P(DP),
    )
    out_specs = (P(DP, CTX, None), P(DP, CTX, None), P(DP, CTX))
    return jax.shard_map(local, mesh=finer, in_specs=in_specs, out_specs=out_specs, check_vma=False)
```

```python
import functools
import math

import jax
import jax.numpy as jnp
from jax import lax
from jax.experimental import pallas as pl
from jax.experimental.pallas import tpu as pltpu
from jax.sharding import Mesh
from jax.sharding import PartitionSpec as P

DN = 128
DR = 64
DV = 128
C = 512
W = C + DR
NZ = 8
NY = 4
HEADS = 4
NQ = 64
ROWS = NQ * HEADS
BLK = 128
DP = ("x", "core")
CTX = ("z", "y")
MSCALE = 0.1 * math.log(40.0) + 1.0
SCALE = MSCALE * MSCALE / math.sqrt(DN + DR)
NEG_FILL = -1e30
BF = jnp.bfloat16
F32 = jnp.float32
OFFSETS = (4, -3, 3, -2, 2, -1, 1, 0)
GROUPS = ((4,), (-3, 3), (-2, 2, -1, 1, 0))
KEYS = len(OFFSETS) * 2 * BLK
TILE = 256


def swap_pairs():
    pairs = []
    for c in range(2):
        for y in range(NY):
            home = (y >> 1) == c
            pairs.append((c * NY + y, c * NY + y if home else (1 - c) * NY + 3 - y))
    return pairs


def swap(v):
    return lax.ppermute(v, ("core", "y"), swap_pairs())


def other_core(v):
    return lax.ppermute(v, "core", [(0, 1), (1, 0)])


def pair_y(v):
    return lax.ppermute(v, "y", [(i, i ^ 1) for i in range(NY)])


def along_z(v, step):
    return lax.ppermute(v, "z", [(i, (i + step) % NZ) for i in range(NZ)])


def dot(a, b, da=1, db=0):
    return lax.dot_general(a, b, (((da,), (db,)), ((), ())), preferred_element_type=F32)


def vmem(shape, dtype):
    return jax.ShapeDtypeStruct(shape, dtype)


def call(body, out_shape, args, flops, scratch=(), smem=0, mib=32):
    specs = [pl.BlockSpec(memory_space=pltpu.SMEM)] * smem
    specs += [pl.BlockSpec(memory_space=pltpu.VMEM)] * (len(args) - smem)
    size = sum(a.size * a.dtype.itemsize for a in args)
    size += sum(o.size * o.dtype.itemsize for o in out_shape)
    return pl.pallas_call(
        body,
        out_shape=out_shape,
        in_specs=specs,
        out_specs=[pl.BlockSpec(memory_space=pltpu.VMEM)] * len(out_shape),
        scratch_shapes=list(scratch),
        compiler_params=pltpu.CompilerParams(vmem_limit_bytes=mib * 1024 * 1024),
        cost_estimate=pl.CostEstimate(flops=flops, bytes_accessed=size, transcendentals=0),
    )(*args)


def latents_body(both, w, out):
    for h in range(HEADS):
        rows = slice(h * NQ, (h + 1) * NQ)
        nope = both[:, h * (DN + DR) : h * (DN + DR) + DN]
        rope = both[:, h * (DN + DR) + DN : (h + 1) * (DN + DR)]
        at = HEADS * (DN + DR) + h * DV
        grad = both[:, at : at + DV]
        wk = w[:, h * (DN + DV) : h * (DN + DV) + DN]
        wv = w[:, h * (DN + DV) + DN : (h + 1) * (DN + DV)]
        out[rows, :C] = dot(grad, wv, 1, 1).astype(BF)
        out[rows, C : 2 * C] = dot(nope, wk, 1, 1).astype(BF)
        out[rows, 2 * C :] = rope


def scores_body(*refs):
    scal, mine, other = refs[:3]
    keys = refs[3:19]
    outs = refs[19:22]
    kt, stats, s_ref, gp_ref = refs[22:26]
    start, low, z, y_own = scal[0], scal[1], scal[2], scal[3]
    for b in range(16):
        kt[:, b * BLK : (b + 1) * BLK] = keys[b][...]
    for half, qg in ((0, mine), (1, other)):
        rows = slice(half * ROWS, (half + 1) * ROWS)
        q = qg[:, C:]
        g = qg[:, :C]
        for t in range(KEYS // TILE):
            cols = slice(t * TILE, (t + 1) * TILE)
            s_ref[rows, cols] = dot(q, kt[:, cols])
            gp_ref[rows, cols] = dot(g, kt[:C, cols])
    step = 16
    lane = lax.broadcasted_iota(jnp.int32, (step, BLK), 1)
    sub = lax.broadcasted_iota(jnp.int32, (step, 1), 0)
    pos = []
    for d in OFFSETS:
        base = ((z + d + NZ) % NZ) * (NY * BLK)
        pos.append(base + y_own * BLK + lane)
        pos.append(base + (y_own ^ 1) * BLK + lane)

    @pl.loop(0, 2 * ROWS // step)
    def _(i):
        r0 = pl.multiple_of(i * step, step)
        here = pl.ds(r0, step)
        last = start + lax.rem(r0, NQ) + sub
        peak = None
        seen = []
        raw = []
        for b in range(16):
            cols = slice(b * BLK, (b + 1) * BLK)
            ok = (pos[b] >= low) & (pos[b] <= last)
            v = jnp.where(ok, s_ref[here, cols] * SCALE, NEG_FILL)
            s_ref[here, cols] = v
            peak = v if peak is None else jnp.maximum(peak, v)
        m = jnp.max(peak, axis=1, keepdims=True)
        total = jnp.zeros((step, BLK), F32)
        rsum = jnp.zeros((step, BLK), F32)
        for b in range(16):
            cols = slice(b * BLK, (b + 1) * BLK)
            v = s_ref[here, cols]
            e = jnp.where(v > 0.5 * NEG_FILL, jnp.exp(v - m), 0.0)
            s_ref[here, cols] = e
            total = total + e
            rsum = rsum + e * gp_ref[here, cols]
        l = jnp.sum(total, axis=1, keepdims=True)
        rd = jnp.sum(rsum, axis=1, keepdims=True) / jnp.where(l > 0.0, l, 1.0)
        at = 0
        for n, group in enumerate(GROUPS):
            for k in range(2 * len(group)):
                cols = slice(at * BLK, (at + 1) * BLK)
                oc = slice(k * BLK, (k + 1) * BLK)
                e = s_ref[here, cols]
                outs[n][here, oc] = (e * (gp_ref[here, cols] - rd)).astype(BF)
                outs[n][pl.ds(pl.multiple_of(2 * ROWS + r0, step), step), oc] = e.astype(BF)
                at += 1
        stats[here, :] = jnp.where(lane == 0, m, jnp.where(lane == 1, l, rd))


def key_parts(qq, ee, outs):
    for k in range(len(outs) // 2):
        r = dot(qq[...], ee[:, k * TILE : (k + 1) * TILE], 0, 0)
        outs[2 * k][...] = r[:, :BLK].astype(BF)
        outs[2 * k + 1][...] = r[:, BLK:].astype(BF)


def first_body(st, their, mine, other, ee, qq, ws, po, pp):
    step = 64

    def body(rows, trows, qg, qrows):
        m, l, rd = st[rows, 0:1], st[rows, 1:2], st[rows, 2:3]
        m2, l2, rd2 = their[trows, 0:1], their[trows, 1:2], their[trows, 2:3]
        top = jnp.maximum(m, m2)
        a = jnp.exp(m - top)
        a2 = jnp.exp(m2 - top)
        denom = l * a + l2 * a2
        shift = (rd * l * a + rd2 * l2 * a2) / denom - rd
        w = a / denom
        sw = SCALE * w
        q = qg[qrows, C:].astype(F32)
        g = qg[qrows, :C].astype(F32)
        qs = q * sw
        qq[rows, :] = qs.astype(BF)
        qd = qs * shift
        low_rows = pl.ds(pl.multiple_of(rows.start + 2 * ROWS, step), step)
        qq[low_rows, :C] = (g * w - qd[:, :C]).astype(BF)
        qq[low_rows, C:] = (-qd[:, C:]).astype(BF)
        lane = lax.broadcasted_iota(jnp.int32, (step, BLK), 1)
        ws[rows, :] = jnp.where(lane == 0, w, shift)

    for half, qg in ((0, mine), (1, other)):

        @pl.loop(0, ROWS // step)
        def _(i):
            r = pl.multiple_of(i * step, step)
            mine_at = pl.multiple_of(half * ROWS + r, step)
            their_at = pl.multiple_of((1 - half) * ROWS + r, step)
            body(pl.ds(mine_at, step), pl.ds(their_at, step), qg, pl.ds(r, step))

    key_parts(qq, ee, (po, pp))


def parts_body(qq, ee, *outs):
    key_parts(qq, ee, outs)


def query_body(ws, kt, e0, e1, e2, mine, other):
    for half, out in ((0, mine), (1, other)):
        xs = []
        for top in (0, 2 * ROWS):
            rows = slice(top + half * ROWS, top + (half + 1) * ROWS)
            acc = None
            at = 0
            for e in (e0, e1, e2):
                n = e.shape[1]
                r = dot(e[rows, :], kt[:, at : at + n], 1, 1)
                acc = r if acc is None else acc + r
                at += n
            xs.append(acc)
        rows = slice(half * ROWS, (half + 1) * ROWS)
        w = ws[rows, 0:1]
        shift = ws[rows, 1:2]
        out[:, :C] = (w * xs[1][:, :C]).astype(out.dtype)
        out[:, C:] = ((SCALE * w) * (xs[0] - shift * xs[1])).astype(out.dtype)


def tail_body(qo, both, w, gq, terms):
    for h in range(HEADS):
        rows = slice(h * NQ, (h + 1) * NQ)
        o = qo[rows, :C]
        lat = qo[rows, C : 2 * C]
        nope = both[:, h * (DN + DR) : h * (DN + DR) + DN]
        at = HEADS * (DN + DR) + h * DV
        grad = both[:, at : at + DV]
        c0 = h * (DN + DV)
        terms[:, c0 : c0 + DN] = dot(lat, nope, 0, 0).astype(BF)
        terms[:, c0 + DN : c0 + DN + DV] = dot(o, grad, 0, 0).astype(BF)
        q0 = h * (DN + DR)
        gq[:, q0 : q0 + DN] = dot(lat, w[:, c0 : c0 + DN]).astype(BF)
        gq[:, q0 + DN : q0 + DN + DR] = qo[rows, 2 * C :]


def plus(a, b):
    return (a.astype(F32) + b.astype(F32)).astype(BF)


def local(queries, grad_out, latent, latent_up, query_start, key_lengths):
    ndev = NZ * NY
    own_q = queries.shape[1]

    own = swap(latent[0].T)
    both = jnp.concatenate(
        [
            queries.reshape(own_q, ndev, HEADS * (DN + DR)),
            grad_out.reshape(own_q, ndev, HEADS * DV),
        ],
        axis=2,
    )
    both = jnp.moveaxis(both, 1, 0)
    ints = jnp.concatenate([query_start, key_lengths])
    own, both, ints = lax.optimization_barrier((own, both, ints))
    partner = pair_y(own)
    ints = swap(ints)
    start, length = ints[0], ints[1]
    both = lax.all_to_all(both, CTX, 0, 0, tiled=True).reshape(NQ, HEADS * (DN + DR + DV))

    kept = {(0, 0): own, (0, 1): partner}
    for s, first in ((0, own), (1, partner)):
        f = b = first
        for j in (1, 2, 3):
            f = along_z(f, 1)
            b = along_z(b, -1)
            kept[(-j, s)] = f
            kept[(j, s)] = b
        kept[(4, s)] = along_z(f, 1) if s == 0 else along_z(b, -1)

    (qg,) = call(latents_body, [vmem((ROWS, W + C), BF)], (both, latent_up), 270_000_000)
    qg = swap(qg)
    qg_other = other_core(qg)

    zi = lax.axis_index("z")
    yi = lax.axis_index("y")
    ci = lax.axis_index("core")
    y_own = jnp.where((yi >> 1) == ci, yi, 3 - yi)
    low = start + NQ - length
    scal = jnp.stack([start, low, zi, y_own]).astype(jnp.int32)
    keys = [kept[(d, s)] for d in OFFSETS for s in (0, 1)]
    shapes = [vmem((4 * ROWS, 2 * BLK * len(g)), BF) for g in GROUPS]
    shapes += [vmem((W, KEYS), BF), vmem((2 * ROWS, BLK), F32)]
    big = pltpu.VMEM((2 * ROWS, KEYS), F32)
    e0, e1, e2, kt, stats = call(
        scores_body, shapes, (scal, qg, qg_other, *keys), 2_280_000_000, (big, big), smem=1
    )
    theirs = other_core(stats)

    piece = vmem((W, BLK), BF)
    qq, ws, p4o, p4p = call(
        first_body,
        [vmem((4 * ROWS, W), BF), vmem((2 * ROWS, BLK), F32), piece, piece],
        (stats, theirs, qg, qg_other, e0),
        300_000_000,
    )
    part = {(4, 0): p4o, (4, 1): p4p}
    for e, group in ((e1, GROUPS[1]), (e2, GROUPS[2])):
        names = [(d, s) for d in group for s in (0, 1)]
        outs = call(parts_body, [piece] * len(names), (qq, e), 300_000_000 * len(group))
        part.update(zip(names, outs))
    sums = []
    for s in (0, 1):
        f = b = None
        if s == 0:
            f = along_z(part[(4, s)], 1)
        else:
            b = along_z(part[(4, s)], -1)
        for j in (3, 2, 1):
            f = along_z(part[(j, s)] if f is None else plus(part[(j, s)], f), 1)
            b = along_z(part[(-j, s)] if b is None else plus(part[(-j, s)], b), -1)
        sums.append(part[(0, s)].astype(F32) + f.astype(F32) + b.astype(F32))
    total = sums[0] + pair_y(sums[1].astype(BF)).astype(F32)
    key_grad = swap(total.astype(BF)).astype(F32).T

    mine, other = call(
        query_body,
        [vmem((ROWS, W + C), F32), vmem((ROWS, W + C), BF)],
        (ws, kt, e0, e1, e2),
        2_400_000_000,
    )
    qo = swap((mine + other_core(other).astype(F32)).astype(BF))
    gq, terms = call(
        tail_body,
        [vmem((NQ, HEADS * (DN + DR)), BF), vmem((C, HEADS * (DN + DV)), BF)],
        (qo, both, latent_up),
        200_000_000,
    )
    terms = terms.reshape(8, C // 8, HEADS * (DN + DV))
    arrived = lax.all_to_all(terms, DP, 0, 0, tiled=True)
    grad_weights = arrived.astype(F32).sum(axis=0)
    back = lax.all_to_all(gq.reshape(ndev, own_q, HEADS * (DN + DR)), CTX, 0, 0, tiled=True)
    grad_queries = jnp.moveaxis(back, 0, 1).reshape(1, own_q, -1).astype(F32)
    return (grad_queries, key_grad[None], grad_weights)


def solution(mesh):
    finer = Mesh(mesh.devices.reshape(4, 2, NZ, NY), ("x", "core", "z", "y"))
    in_specs = (
        P(DP, CTX, None),
        P(DP, CTX, None),
        P(DP, CTX, None),
        P(None, CTX),
        P(DP),
        P(DP),
    )
    out_specs = (P(DP, CTX, None), P(DP, CTX, None), P(DP, CTX))
    return jax.shard_map(local, mesh=finer, in_specs=in_specs, out_specs=out_specs, check_vma=False)
```

```python
import math

import jax
import jax.numpy as jnp
from jax import lax
from jax.experimental import pallas as pl
from jax.experimental.pallas import tpu as pltpu
from jax.sharding import Mesh
from jax.sharding import PartitionSpec as P


DN = 128
DR = 64
DV = 128
C = 512
W = C + DR
NZ = 8
NY = 4
HEADS = 4
NQ = 64
ROWS = NQ * HEADS
WIDE = 2 * C + 2 * DR
BLK = 128
DP = ("x", "core")
CTX = ("z", "y")
MSCALE = 0.1 * math.log(40.0) + 1.0
SCALE = MSCALE * MSCALE / math.sqrt(DN + DR)
NEG_FILL = -1e30
BF = jnp.bfloat16
F32 = jnp.float32
OFFSETS = (0, 4, -3, 3, -2, 2, -1, 1)
KEYS = 2 * NZ * BLK
TILE = 256


def turned(flip):
    pairs = []
    for c in range(2):
        for y in range(NY):
            v, w = y >> 1, y & 1
            pairs.append((c * NY + y, v * NY + 2 * c + (w ^ flip)))
    return pairs


def swap_pairs():
    pairs = []
    for c in range(2):
        for y in range(NY):
            home = (y >> 1) == c
            pairs.append((c * NY + y, c * NY + y if home else (1 - c) * NY + 3 - y))
    return pairs


def swap(v):
    return lax.ppermute(v, ("core", "y"), swap_pairs())


def turn(v, flip):
    return lax.ppermute(v, ("core", "y"), turned(flip))


def other_core(v):
    return lax.ppermute(v, "core", [(0, 1), (1, 0)])


def pair_y(v):
    return lax.ppermute(v, "y", [(i, i ^ 1) for i in range(NY)])


def along_z(v, step):
    return lax.ppermute(v, "z", [(i, (i + step) % NZ) for i in range(NZ)])


def dot(a, b, da=1, db=0):
    return lax.dot_general(a, b, (((da,), (db,)), ((), ())), preferred_element_type=F32)


def vmem(shape, dtype):
    return jax.ShapeDtypeStruct(shape, dtype)


def call(body, out_shape, args, flops, scratch=(), smem=0, mib=32):
    specs = [pl.BlockSpec(memory_space=pltpu.SMEM)] * smem
    specs += [pl.BlockSpec(memory_space=pltpu.VMEM)] * (len(args) - smem)
    size = sum(a.size * a.dtype.itemsize for a in args)
    size += sum(o.size * o.dtype.itemsize for o in out_shape)
    return pl.pallas_call(
        body,
        out_shape=out_shape,
        in_specs=specs,
        out_specs=[pl.BlockSpec(memory_space=pltpu.VMEM)] * len(out_shape),
        scratch_shapes=list(scratch),
        compiler_params=pltpu.CompilerParams(vmem_limit_bytes=mib * 1024 * 1024),
        cost_estimate=pl.CostEstimate(flops=flops, bytes_accessed=size, transcendentals=0),
    )(*args)


def latents_body(start, length, both, w, out):
    lane = lax.broadcasted_iota(jnp.int32, (NQ, DR), 1)
    note = jnp.zeros((NQ, DR), F32)
    low = start[0] + NQ - length[0]
    for n, v in enumerate((start[0] // NQ, start[0] % NQ, low // NQ, low % NQ)):
        note = jnp.where(lane == n, v.astype(F32), note)
    note = note.astype(BF)
    for h in range(HEADS):
        rows = slice(h * NQ, (h + 1) * NQ)
        nope = both[:, h * (DN + DR) : h * (DN + DR) + DN]
        rope = both[:, h * (DN + DR) + DN : (h + 1) * (DN + DR)]
        at = HEADS * (DN + DR) + h * DV
        grad = both[:, at : at + DV]
        wk = w[:, h * (DN + DV) : h * (DN + DV) + DN]
        wv = w[:, h * (DN + DV) + DN : (h + 1) * (DN + DV)]
        out[rows, :C] = dot(grad, wv, 1, 1).astype(BF)
        out[rows, C : 2 * C] = dot(nope, wk, 1, 1).astype(BF)
        out[rows, 2 * C : C + W] = rope
        out[rows, C + W :] = note


def join_body(*refs):
    for b in range(NZ):
        refs[NZ][:, b * BLK : (b + 1) * BLK] = refs[b][...]


def scores_body(*refs):
    scal, mine, other = refs[:3]
    keys = refs[3:5]
    e_mine, e_their, kt, stats, s_ref, gp_ref = refs[5:]
    z, y_own = scal[0], scal[1]
    for n in range(2):
        kt[:, n * NZ * BLK : (n + 1) * NZ * BLK] = keys[n][...]
    for half, qg in ((0, mine), (1, other)):
        rows = slice(half * ROWS, (half + 1) * ROWS)
        q = qg[:, C : C + W]
        g = qg[:, :C]
        for t in range(KEYS // TILE):
            cols = slice(t * TILE, (t + 1) * TILE)
            s_ref[rows, cols] = dot(q, kt[:, cols])
            gp_ref[rows, cols] = dot(g, kt[:C, cols])
    step = 16
    lane = lax.broadcasted_iota(jnp.int32, (step, BLK), 1)
    sub = lax.broadcasted_iota(jnp.int32, (step, 1), 0)
    pos = []
    for y in (y_own, 3 - y_own):
        for d in OFFSETS:
            pos.append(((z + d + NZ) % NZ) * (NY * BLK) + y * BLK + lane)

    @pl.loop(0, 2 * ROWS // step)
    def _(i):
        r0 = pl.multiple_of(i * step, step)
        here = pl.ds(r0, step)
        below = pl.ds(pl.multiple_of(2 * ROWS + r0, step), step)
        note = mine[pl.ds(pl.multiple_of(lax.rem(r0, ROWS), step), step), 2 * C :].astype(F32)
        note = note.astype(jnp.int32)
        start = note[:, DR : DR + 1] * NQ + note[:, DR + 1 : DR + 2]
        low = note[:, DR + 2 : DR + 3] * NQ + note[:, DR + 3 : DR + 4]
        last = start + lax.rem(r0, NQ) + sub
        peak = None
        for b in range(16):
            cols = slice(b * BLK, (b + 1) * BLK)
            ok = (pos[b] >= low) & (pos[b] <= last)
            v = jnp.where(ok, s_ref[here, cols] * SCALE, NEG_FILL)
            s_ref[here, cols] = v
            peak = v if peak is None else jnp.maximum(peak, v)
        m = jnp.max(peak, axis=1, keepdims=True)
        total = jnp.zeros((step, BLK), F32)
        rsum = jnp.zeros((step, BLK), F32)
        for b in range(16):
            cols = slice(b * BLK, (b + 1) * BLK)
            v = s_ref[here, cols]
            e = jnp.where(v > 0.5 * NEG_FILL, jnp.exp(v - m), 0.0)
            s_ref[here, cols] = e
            total = total + e
            rsum = rsum + e * gp_ref[here, cols]
        l = jnp.sum(total, axis=1, keepdims=True)
        rd = jnp.sum(rsum, axis=1, keepdims=True) / jnp.where(l > 0.0, l, 1.0)
        for b in range(16):
            cols = slice(b * BLK, (b + 1) * BLK)
            out = e_mine if b < 8 else e_their
            oc = slice((b % 8) * BLK, (b % 8 + 1) * BLK)
            e = s_ref[here, cols]
            out[here, oc] = (e * (gp_ref[here, cols] - rd)).astype(BF)
            out[below, oc] = e.astype(BF)
        stats[here, :] = jnp.where(lane == 0, m, jnp.where(lane == 1, l, rd))


def key_parts(qq, ee, out):
    for k in range(NZ // 2):
        r = dot(qq[...], ee[:, k * TILE : (k + 1) * TILE], 0, 0)
        for n in range(2):
            out[2 * k + n] = r[:, n * BLK : (n + 1) * BLK].astype(BF)


def add_body(a, b, *outs):
    for k in range(NZ):
        outs[k][...] = (a[k].astype(F32) + b[k].astype(F32)).astype(BF)


def total_body(*refs):
    acc = refs[0][...].astype(F32)
    for k in range(1, NZ):
        acc = acc + refs[k][...].astype(F32)
    refs[NZ][...] = acc.astype(BF)


def first_body(st, their, mine, other, ee, qq, ws, out):
    step = 64

    def body(rows, trows, qg, qrows):
        m, l, rd = st[rows, 0:1], st[rows, 1:2], st[rows, 2:3]
        m2, l2, rd2 = their[trows, 0:1], their[trows, 1:2], their[trows, 2:3]
        top = jnp.maximum(m, m2)
        a = jnp.exp(m - top)
        a2 = jnp.exp(m2 - top)
        denom = l * a + l2 * a2
        shift = (rd * l * a + rd2 * l2 * a2) / denom - rd
        w = a / denom
        sw = SCALE * w
        q = qg[qrows, C : C + W].astype(F32)
        g = qg[qrows, :C].astype(F32)
        qs = q * sw
        qq[rows, :] = qs.astype(BF)
        qd = qs * shift
        low_rows = pl.ds(pl.multiple_of(rows.start + 2 * ROWS, step), step)
        qq[low_rows, :C] = (g * w - qd[:, :C]).astype(BF)
        qq[low_rows, C:] = (-qd[:, C:]).astype(BF)
        lane = lax.broadcasted_iota(jnp.int32, (step, BLK), 1)
        ws[rows, :] = jnp.where(lane == 0, w, shift)

    for half, qg in ((0, mine), (1, other)):

        @pl.loop(0, ROWS // step)
        def _(i):
            r = pl.multiple_of(i * step, step)
            mine_at = pl.multiple_of(half * ROWS + r, step)
            their_at = pl.multiple_of((1 - half) * ROWS + r, step)
            body(pl.ds(mine_at, step), pl.ds(their_at, step), qg, pl.ds(r, step))

    key_parts(qq, ee, out)


def parts_body(qq, ee, out):
    key_parts(qq, ee, out)


def query_body(ws, kt, e0, e1, mine, other):
    for half, out in ((0, mine), (1, other)):
        xs = []
        for top in (0, 2 * ROWS):
            rows = slice(top + half * ROWS, top + (half + 1) * ROWS)
            acc = None
            at = 0
            for e in (e0, e1):
                n = e.shape[1]
                r = dot(e[rows, :], kt[:, at : at + n], 1, 1)
                acc = r if acc is None else acc + r
                at += n
            xs.append(acc)
        rows = slice(half * ROWS, (half + 1) * ROWS)
        w = ws[rows, 0:1]
        shift = ws[rows, 1:2]
        out[:, :C] = (w * xs[1][:, :C]).astype(out.dtype)
        out[:, C : C + W] = ((SCALE * w) * (xs[0] - shift * xs[1])).astype(out.dtype)
        out[:, C + W :] = jnp.zeros((ROWS, DR), out.dtype)


def tail_body(scal, qo, both, w, gq, keep, send, terms):
    for h in range(HEADS):
        rows = slice(h * NQ, (h + 1) * NQ)
        o = qo[rows, :C]
        lat = qo[rows, C : 2 * C]
        nope = both[:, h * (DN + DR) : h * (DN + DR) + DN]
        at = HEADS * (DN + DR) + h * DV
        grad = both[:, at : at + DV]
        c0 = h * (DN + DV)
        terms[:, c0 : c0 + DN] = dot(lat, nope, 0, 0).astype(BF)
        terms[:, c0 + DN : c0 + DN + DV] = dot(o, grad, 0, 0).astype(BF)
        q0 = h * (DN + DR)
        gq[:, q0 : q0 + DN] = dot(lat, w[:, c0 : c0 + DN]).astype(BF)
        gq[:, q0 + DN : q0 + DN + DR] = qo[rows, 2 * C : C + W]
    x, c = scal[2], scal[3]
    n = C // 8
    for k in range(4):
        base = lax.rem(x + k, 4) * (2 * n)
        slot = slice(k * n, (k + 1) * n)
        keep[slot, :] = terms[pl.ds(pl.multiple_of(base + c * n, n), n), :]
        send[slot, :] = terms[pl.ds(pl.multiple_of(base + (1 - c) * n, n), n), :]


def step(queries, grad_out, latent, latent_up, query_start, key_lengths):
    ndev = NZ * NY
    own_q = queries.shape[1]

    own = swap(latent[0].T)
    both = jnp.concatenate(
        [
            queries.reshape(own_q, ndev, HEADS * (DN + DR)),
            grad_out.reshape(own_q, ndev, HEADS * DV),
        ],
        axis=2,
    )
    both = jnp.moveaxis(both, 1, 0)
    both = lax.all_to_all(both, CTX, 0, 0, tiled=True)
    both = both.reshape(NQ, HEADS * (DN + DR + DV))

    kept = [own] + [along_z(own, -d) for d in OFFSETS[1:]]

    (qg,) = call(
        latents_body,
        [vmem((ROWS, WIDE), BF)],
        (query_start, key_lengths, both, latent_up),
        270_000_000,
        smem=2,
    )
    qg_mine = turn(qg, 0)
    qg_other = turn(qg, 1)
    (mine_side,) = call(join_body, [vmem((W, NZ * BLK), BF)], kept, 1_000_000)
    their_side = other_core(mine_side)

    zi = lax.axis_index("z")
    yi = lax.axis_index("y")
    ci = lax.axis_index("core")
    y_own = jnp.where((yi >> 1) == ci, yi, 3 - yi)
    scal = jnp.stack([zi, y_own, lax.axis_index("x"), ci]).astype(jnp.int32)
    half = vmem((4 * ROWS, NZ * BLK), BF)
    big = pltpu.VMEM((2 * ROWS, KEYS), F32)
    e_mine, e_their, kt, stats = call(
        scores_body,
        [half, half, vmem((W, KEYS), BF), vmem((2 * ROWS, BLK), F32)],
        (scal, qg_mine, qg_other, mine_side, their_side),
        2_280_000_000,
        (big, big),
        smem=1,
    )
    theirs = pair_y(stats)

    piece = vmem((NZ, W, BLK), BF)
    qq, ws, their_keys = call(
        first_body,
        [vmem((4 * ROWS, W), BF), vmem((2 * ROWS, BLK), F32), piece],
        (stats, theirs, qg_mine, qg_other, e_their),
        1_300_000_000,
    )
    their_keys = other_core(their_keys)
    (mine_keys,) = call(parts_body, [piece], (qq, e_mine), 1_200_000_000)
    sums = call(add_body, [vmem((W, BLK), BF)] * NZ, (mine_keys, their_keys), 1_000_000)
    sums, ws = lax.optimization_barrier((sums, ws))
    sums = [sums[0]] + [along_z(sums[n + 1], d) for n, d in enumerate(OFFSETS[1:])]
    (total,) = call(total_body, [vmem((W, BLK), BF)], sums, 1_000_000)
    key_grad = swap(total).astype(F32).T

    mine, other = call(
        query_body,
        [vmem((ROWS, WIDE), BF), vmem((ROWS, WIDE), BF)],
        (ws, kt, e_mine, e_their),
        2_400_000_000,
    )
    qo = (turn(mine, 0).astype(F32) + turn(other, 1).astype(F32)).astype(BF)
    wide = HEADS * (DN + DV)
    gq, keep, send = call(
        tail_body,
        [vmem((NQ, HEADS * (DN + DR)), BF)] + [vmem((C // 2, wide), BF)] * 2,
        (scal, qo, both, latent_up),
        200_000_000,
        (pltpu.VMEM((C, wide), BF),),
        smem=1,
    )
    got = other_core(send)
    n = C // 8
    grad_weights = keep[:n].astype(F32) + got[:n].astype(F32)
    for k in range(1, 4):
        rows = slice(k * n, (k + 1) * n)
        pair = (keep[rows].astype(F32) + got[rows].astype(F32)).astype(BF)
        pair = lax.ppermute(pair, "x", [(i, (i + k) % 4) for i in range(4)])
        grad_weights = grad_weights + pair.astype(F32)
    back = lax.all_to_all(gq.reshape(ndev, own_q, HEADS * (DN + DR)), CTX, 0, 0, tiled=True)
    grad_queries = jnp.moveaxis(back, 0, 1).reshape(1, own_q, -1).astype(F32)
    return (grad_queries, key_grad[None], grad_weights)


def solution(mesh):
    finer = Mesh(mesh.devices.reshape(4, 2, NZ, NY), ("x", "core", "z", "y"))
    in_specs = (
        P(DP, CTX, None),
        P(DP, CTX, None),
        P(DP, CTX, None),
        P(None, CTX),
        P(DP),
        P(DP),
    )
    out_specs = (P(DP, CTX, None), P(DP, CTX, None), P(DP, CTX))
    return jax.shard_map(step, mesh=finer, in_specs=in_specs, out_specs=out_specs, check_vma=False)
```

```python
import math

import jax
import jax.numpy as jnp
from jax import lax
from jax.experimental import pallas as pl
from jax.experimental.pallas import tpu as pltpu
from jax.sharding import Mesh
from jax.sharding import PartitionSpec as P


DN = 128
DR = 64
DV = 128
C = 512
W = C + DR
NZ = 8
NY = 4
HEADS = 4
NQ = 64
ROWS = NQ * HEADS
WIDE = 2 * C + 2 * DR
BLK = 128
DP = ("x", "core")
CTX = ("z", "y")
MSCALE = 0.1 * math.log(40.0) + 1.0
SCALE = MSCALE * MSCALE / math.sqrt(DN + DR)
NEG_FILL = -1e30
BF = jnp.bfloat16
F32 = jnp.float32
OFFSETS = (0, 4, -3, 3, -2, 2, -1, 1)
KEYS = 2 * NZ * BLK
TILE = 256


def turned(flip):
    pairs = []
    for c in range(2):
        for y in range(NY):
            v, w = y >> 1, y & 1
            pairs.append((c * NY + y, v * NY + 2 * c + (w ^ flip)))
    return pairs


def swap_pairs():
    pairs = []
    for c in range(2):
        for y in range(NY):
            home = (y >> 1) == c
            pairs.append((c * NY + y, c * NY + y if home else (1 - c) * NY + 3 - y))
    return pairs


def swap(v):
    return lax.ppermute(v, ("core", "y"), swap_pairs())


def turn(v, flip):
    return lax.ppermute(v, ("core", "y"), turned(flip))


def other_core(v):
    return lax.ppermute(v, "core", [(0, 1), (1, 0)])


def pair_y(v):
    return lax.ppermute(v, "y", [(i, i ^ 1) for i in range(NY)])


def along_z(v, step):
    return lax.ppermute(v, "z", [(i, (i + step) % NZ) for i in range(NZ)])


def dot(a, b, da=1, db=0):
    return lax.dot_general(a, b, (((da,), (db,)), ((), ())), preferred_element_type=F32)


def vmem(shape, dtype):
    return jax.ShapeDtypeStruct(shape, dtype)


def call(body, out_shape, args, flops, scratch=(), smem=0, mib=32):
    specs = [pl.BlockSpec(memory_space=pltpu.SMEM)] * smem
    specs += [pl.BlockSpec(memory_space=pltpu.VMEM)] * (len(args) - smem)
    size = sum(a.size * a.dtype.itemsize for a in args)
    size += sum(o.size * o.dtype.itemsize for o in out_shape)
    return pl.pallas_call(
        body,
        out_shape=out_shape,
        in_specs=specs,
        out_specs=[pl.BlockSpec(memory_space=pltpu.VMEM)] * len(out_shape),
        scratch_shapes=list(scratch),
        compiler_params=pltpu.CompilerParams(vmem_limit_bytes=mib * 1024 * 1024),
        cost_estimate=pl.CostEstimate(flops=flops, bytes_accessed=size, transcendentals=0),
    )(*args)


def latents_body(start, length, both, w, out):
    lane = lax.broadcasted_iota(jnp.int32, (NQ, DR), 1)
    note = jnp.zeros((NQ, DR), F32)
    low = start[0] + NQ - length[0]
    for n, v in enumerate((start[0] // NQ, start[0] % NQ, low // NQ, low % NQ)):
        note = jnp.where(lane == n, v.astype(F32), note)
    note = note.astype(BF)
    for h in range(HEADS):
        rows = slice(h * NQ, (h + 1) * NQ)
        nope = both[:, h * (DN + DR) : h * (DN + DR) + DN]
        rope = both[:, h * (DN + DR) + DN : (h + 1) * (DN + DR)]
        at = HEADS * (DN + DR) + h * DV
        grad = both[:, at : at + DV]
        wk = w[:, h * (DN + DV) : h * (DN + DV) + DN]
        wv = w[:, h * (DN + DV) + DN : (h + 1) * (DN + DV)]
        out[rows, :C] = dot(grad, wv, 1, 1).astype(BF)
        out[rows, C : 2 * C] = dot(nope, wk, 1, 1).astype(BF)
        out[rows, 2 * C : C + W] = rope
        out[rows, C + W :] = note


def join_body(*refs):
    for b in range(NZ):
        refs[NZ][:, b * BLK : (b + 1) * BLK] = refs[b][...]


def scores_body(*refs):
    scal, mine, other = refs[:3]
    keys = refs[3:5]
    e_mine, e_their, kt, stats, s_ref, gp_ref, wide = refs[5:]
    z, y_own = scal[0], scal[1]
    for n in range(2):
        kt[:, n * NZ * BLK : (n + 1) * NZ * BLK] = keys[n][...]
    note = mine[0:16, 2 * C :].astype(F32).astype(jnp.int32)[0:8, :]
    start = note[:, DR : DR + 1] * NQ + note[:, DR + 1 : DR + 2]
    low = note[:, DR + 2 : DR + 3] * NQ + note[:, DR + 3 : DR + 4]
    lane = lax.broadcasted_iota(jnp.int32, (8, BLK), 1)
    sub = lax.broadcasted_iota(jnp.int32, (8, BLK), 0)
    above = lane - low
    ahead = lane - start - sub
    base = []
    for y in (y_own, 3 - y_own):
        for d in OFFSETS:
            base.append(((z + d + NZ) % NZ) * (NY * BLK) + y * BLK)
    for half, qg in ((0, mine), (1, other)):
        rows = slice(half * ROWS, (half + 1) * ROWS)
        q = qg[:, C : C + W]
        g = qg[:, :C]
        for t in range(KEYS // TILE):
            cols = slice(t * TILE, (t + 1) * TILE)
            s_ref[rows, cols] = dot(q, kt[:, cols])
            gp_ref[rows, cols] = dot(g, kt[:C, cols])
    chunk = NQ

    @pl.loop(0, 2 * ROWS // chunk)
    def _(i):
        r0 = pl.multiple_of(i * chunk, chunk)
        here = pl.ds(r0, chunk)
        below = pl.ds(pl.multiple_of(2 * ROWS + r0, chunk), chunk)
        peak = [None] * (chunk // 8)
        for b in range(16):
            cols = slice(b * BLK, (b + 1) * BLK)
            inside = above + base[b] >= 0
            gap = ahead + base[b]
            for k in range(chunk // 8):
                r = pl.ds(pl.multiple_of(r0 + 8 * k, 8), 8)
                ok = inside & (gap <= 8 * k)
                v = jnp.where(ok, s_ref[r, cols] * SCALE, NEG_FILL)
                s_ref[r, cols] = v
                peak[k] = v if peak[k] is None else jnp.maximum(peak[k], v)
        m = jnp.max(jnp.concatenate(peak, axis=0), axis=1, keepdims=True)
        safe = jnp.broadcast_to(jnp.maximum(m, 0.1 * NEG_FILL), (chunk, BLK))
        total = None
        rsum = None
        for b in range(16):
            cols = slice(b * BLK, (b + 1) * BLK)
            e = jnp.exp(s_ref[here, cols] - safe)
            s_ref[here, cols] = e
            p = e * gp_ref[here, cols]
            total = e if total is None else total + e
            rsum = p if rsum is None else rsum + p
        l = jnp.sum(total, axis=1, keepdims=True)
        rd = jnp.sum(rsum, axis=1, keepdims=True) / jnp.where(l > 0.0, l, 1.0)
        rdb = jnp.broadcast_to(rd, (chunk, BLK))
        for b in range(16):
            cols = slice(b * BLK, (b + 1) * BLK)
            out = e_mine if b < 8 else e_their
            oc = slice((b % 8) * BLK, (b % 8 + 1) * BLK)
            e = s_ref[here, cols]
            out[here, oc] = (e * (gp_ref[here, cols] - rdb)).astype(BF)
            out[below, oc] = e.astype(BF)
        col = lax.broadcasted_iota(jnp.int32, (chunk, BLK), 1)
        wide[here, :] = jnp.where(col == 0, m, jnp.where(col == 1, l, rd))

    stats[...] = jnp.transpose(wide[...])[0:8, :]


def key_parts(qq, ee, out):
    for k in range(NZ // 2):
        r = dot(qq[...], ee[:, k * TILE : (k + 1) * TILE], 0, 0)
        for n in range(2):
            out[2 * k + n] = r[:, n * BLK : (n + 1) * BLK].astype(BF)


def add_body(a, b, *outs):
    for k in range(NZ):
        outs[k][...] = (a[k].astype(F32) + b[k].astype(F32)).astype(BF)


def total_body(*refs):
    acc = refs[0][...].astype(F32)
    for k in range(1, NZ):
        acc = acc + refs[k][...].astype(F32)
    refs[NZ][...] = acc.astype(BF)


def first_body(st, their, mine, other, ee, qq, ws, out):
    there = jnp.concatenate([their[:, ROWS:], their[:, :ROWS]], axis=1)
    m, l, rd = st[0:1, :], st[1:2, :], st[2:3, :]
    m2, l2, rd2 = there[0:1, :], there[1:2, :], there[2:3, :]
    top = jnp.maximum(m, m2)
    a = jnp.exp(m - top)
    a2 = jnp.exp(m2 - top)
    denom = l * a + l2 * a2
    shift = (rd * l * a + rd2 * l2 * a2) / denom - rd
    w = a / denom
    row = lax.broadcasted_iota(jnp.int32, (BLK, 2 * ROWS), 0)
    ws[...] = jnp.transpose(jnp.where(row == 0, w, shift))
    step = 64
    for half, qg in ((0, mine), (1, other)):

        @pl.loop(0, ROWS // step)
        def _(i):
            r = pl.multiple_of(i * step, step)
            at = pl.multiple_of(half * ROWS + r, step)
            rows = pl.ds(at, step)
            below = pl.ds(pl.multiple_of(at + 2 * ROWS, step), step)
            wv = ws[rows, 0:1]
            dv = ws[rows, 1:2]
            q = qg[pl.ds(r, step), C : C + W].astype(F32)
            g = qg[pl.ds(r, step), :C].astype(F32)
            qs = q * (SCALE * wv)
            qq[rows, :] = qs.astype(BF)
            qd = qs * dv
            qq[below, :C] = (g * wv - qd[:, :C]).astype(BF)
            qq[below, C:] = (-qd[:, C:]).astype(BF)

    key_parts(qq, ee, out)


def parts_body(qq, ee, out):
    key_parts(qq, ee, out)


def query_body(ws, kt, e0, e1, mine, other):
    for half, out in ((0, mine), (1, other)):
        xs = []
        for top in (0, 2 * ROWS):
            rows = slice(top + half * ROWS, top + (half + 1) * ROWS)
            acc = None
            at = 0
            for e in (e0, e1):
                n = e.shape[1]
                r = dot(e[rows, :], kt[:, at : at + n], 1, 1)
                acc = r if acc is None else acc + r
                at += n
            xs.append(acc)
        rows = slice(half * ROWS, (half + 1) * ROWS)
        w = ws[rows, 0:1]
        shift = ws[rows, 1:2]
        out[:, :C] = (w * xs[1][:, :C]).astype(out.dtype)
        out[:, C : C + W] = ((SCALE * w) * (xs[0] - shift * xs[1])).astype(out.dtype)
        out[:, C + W :] = jnp.zeros((ROWS, DR), out.dtype)


def tail_body(scal, qo, both, w, gq, keep, send, terms):
    for h in range(HEADS):
        rows = slice(h * NQ, (h + 1) * NQ)
        o = qo[rows, :C]
        lat = qo[rows, C : 2 * C]
        nope = both[:, h * (DN + DR) : h * (DN + DR) + DN]
        at = HEADS * (DN + DR) + h * DV
        grad = both[:, at : at + DV]
        c0 = h * (DN + DV)
        terms[:, c0 : c0 + DN] = dot(lat, nope, 0, 0).astype(BF)
        terms[:, c0 + DN : c0 + DN + DV] = dot(o, grad, 0, 0).astype(BF)
        q0 = h * (DN + DR)
        gq[:, q0 : q0 + DN] = dot(lat, w[:, c0 : c0 + DN]).astype(BF)
        gq[:, q0 + DN : q0 + DN + DR] = qo[rows, 2 * C : C + W]
    x, c = scal[2], scal[3]
    n = C // 8
    for k in range(4):
        base = lax.rem(x + k, 4) * (2 * n)
        slot = slice(k * n, (k + 1) * n)
        keep[slot, :] = terms[pl.ds(pl.multiple_of(base + c * n, n), n), :]
        send[slot, :] = terms[pl.ds(pl.multiple_of(base + (1 - c) * n, n), n), :]


def step(queries, grad_out, latent, latent_up, query_start, key_lengths):
    ndev = NZ * NY
    own_q = queries.shape[1]

    own = swap(latent[0].T)
    both = jnp.concatenate(
        [
            queries.reshape(own_q, ndev, HEADS * (DN + DR)),
            grad_out.reshape(own_q, ndev, HEADS * DV),
        ],
        axis=2,
    )
    both = jnp.moveaxis(both, 1, 0)
    both = lax.all_to_all(both, CTX, 0, 0, tiled=True)
    both = both.reshape(NQ, HEADS * (DN + DR + DV))

    kept = [own] + [along_z(own, -d) for d in OFFSETS[1:]]

    (qg,) = call(
        latents_body,
        [vmem((ROWS, WIDE), BF)],
        (query_start, key_lengths, both, latent_up),
        270_000_000,
        smem=2,
    )
    qg_mine = turn(qg, 0)
    qg_other = turn(qg, 1)
    (mine_side,) = call(join_body, [vmem((W, NZ * BLK), BF)], kept, 1_000_000)
    their_side = other_core(mine_side)

    zi = lax.axis_index("z")
    yi = lax.axis_index("y")
    ci = lax.axis_index("core")
    y_own = jnp.where((yi >> 1) == ci, yi, 3 - yi)
    scal = jnp.stack([zi, y_own, lax.axis_index("x"), ci]).astype(jnp.int32)
    half = vmem((4 * ROWS, NZ * BLK), BF)
    big = pltpu.VMEM((2 * ROWS, KEYS), F32)
    e_mine, e_their, kt, stats = call(
        scores_body,
        [half, half, vmem((W, KEYS), BF), vmem((8, 2 * ROWS), F32)],
        (scal, qg_mine, qg_other, mine_side, their_side),
        2_280_000_000,
        (big, big, pltpu.VMEM((2 * ROWS, BLK), F32)),
        smem=1,
    )
    theirs = pair_y(stats)

    piece = vmem((NZ, W, BLK), BF)
    qq, ws, their_keys = call(
        first_body,
        [vmem((4 * ROWS, W), BF), vmem((2 * ROWS, BLK), F32), piece],
        (stats, theirs, qg_mine, qg_other, e_their),
        1_300_000_000,
    )
    their_keys = other_core(their_keys)
    (mine_keys,) = call(parts_body, [piece], (qq, e_mine), 1_200_000_000)
    sums = call(add_body, [vmem((W, BLK), BF)] * NZ, (mine_keys, their_keys), 1_000_000)
    sums, ws = lax.optimization_barrier((sums, ws))
    moved = [sums[0]]
    for n, d in enumerate(OFFSETS[1:]):
        moved.append(along_z(sums[n + 1], d))
    (total,) = call(total_body, [vmem((W, BLK), BF)], moved, 1_000_000)
    key_grad = swap(total).astype(F32).T

    mine, other = call(
        query_body,
        [vmem((ROWS, WIDE), BF), vmem((ROWS, WIDE), BF)],
        (ws, kt, e_mine, e_their),
        2_400_000_000,
    )
    mine, other = turn(mine, 0), turn(other, 1)
    qo = (mine.astype(F32) + other.astype(F32)).astype(BF)
    wide = HEADS * (DN + DV)
    gq, keep, send = call(
        tail_body,
        [vmem((NQ, HEADS * (DN + DR)), BF)] + [vmem((C // 2, wide), BF)] * 2,
        (scal, qo, both, latent_up),
        200_000_000,
        (pltpu.VMEM((C, wide), BF),),
        smem=1,
    )
    got = other_core(send)
    n = C // 8
    grad_weights = keep[:n].astype(F32) + got[:n].astype(F32)
    for k in range(1, 4):
        rows = slice(k * n, (k + 1) * n)
        pair = (keep[rows].astype(F32) + got[rows].astype(F32)).astype(BF)
        pair = lax.ppermute(pair, "x", [(i, (i + k) % 4) for i in range(4)])
        grad_weights = grad_weights + pair.astype(F32)
    back = lax.all_to_all(gq.reshape(ndev, own_q, HEADS * (DN + DR)), CTX, 0, 0, tiled=True)
    grad_queries = jnp.moveaxis(back, 0, 1).reshape(1, own_q, -1).astype(F32)
    return (grad_queries, key_grad[None], grad_weights)


def solution(mesh):
    finer = Mesh(mesh.devices.reshape(4, 2, NZ, NY), ("x", "core", "z", "y"))
    in_specs = (
        P(DP, CTX, None),
        P(DP, CTX, None),
        P(DP, CTX, None),
        P(None, CTX),
        P(DP),
        P(DP),
    )
    out_specs = (P(DP, CTX, None), P(DP, CTX, None), P(DP, CTX))
    return jax.shard_map(step, mesh=finer, in_specs=in_specs, out_specs=out_specs, check_vma=False)
```

```python
import math

import jax
import jax.numpy as jnp
from jax import lax
from jax.experimental import pallas as pl
from jax.experimental.pallas import tpu as pltpu
from jax.sharding import Mesh
from jax.sharding import PartitionSpec as P


DN = 128
DR = 64
DV = 128
C = 512
W = C + DR
NZ = 8
NY = 4
HEADS = 4
NQ = 64
ROWS = NQ * HEADS
WIDE = 2 * C + 2 * DR
RAW = HEADS * (DN + DR + DV)
BLK = 128
DP = ("x", "core")
CTX = ("z", "y")
MSCALE = 0.1 * math.log(40.0) + 1.0
SCALE = MSCALE * MSCALE / math.sqrt(DN + DR)
NEG_FILL = -1e30
BF = jnp.bfloat16
F32 = jnp.float32
OFFSETS = (0, 4, -3, 3, -2, 2, -1, 1)
KEYS = 2 * NZ * BLK
TILE = 256


def turned(flip):
    pairs = []
    for c in range(2):
        for y in range(NY):
            v, w = y >> 1, y & 1
            pairs.append((c * NY + y, v * NY + 2 * c + (w ^ flip)))
    return pairs


def swap_pairs():
    pairs = []
    for c in range(2):
        for y in range(NY):
            home = (y >> 1) == c
            pairs.append((c * NY + y, c * NY + y if home else (1 - c) * NY + 3 - y))
    return pairs


def swap(v):
    return lax.ppermute(v, ("core", "y"), swap_pairs())


def turn(v, flip):
    return lax.ppermute(v, ("core", "y"), turned(flip))


def relay(v):
    pairs = []
    for c in range(2):
        for y in range(NY):
            away = int((y >> 1) != c)
            pairs.append((c * NY + y, c * NY + (y ^ away)))
    return lax.ppermute(v, ("core", "y"), pairs)


def other_core(v):
    return lax.ppermute(v, "core", [(0, 1), (1, 0)])


def pair_y(v):
    return lax.ppermute(v, "y", [(i, i ^ 1) for i in range(NY)])


def along_z(v, step):
    return lax.ppermute(v, "z", [(i, (i + step) % NZ) for i in range(NZ)])


def dot(a, b, da=1, db=0):
    return lax.dot_general(a, b, (((da,), (db,)), ((), ())), preferred_element_type=F32)


def in_hbm(v):
    return pltpu.with_memory_space_constraint(v, pltpu.HBM)


def vmem(shape, dtype):
    return jax.ShapeDtypeStruct(shape, dtype)


def call(body, out_shape, args, flops, scratch=(), smem=0, mib=32):
    specs = [pl.BlockSpec(memory_space=pltpu.SMEM)] * smem
    specs += [pl.BlockSpec(memory_space=pltpu.VMEM)] * (len(args) - smem)
    size = sum(a.size * a.dtype.itemsize for a in args)
    size += sum(o.size * o.dtype.itemsize for o in out_shape)
    return pl.pallas_call(
        body,
        out_shape=out_shape,
        in_specs=specs,
        out_specs=[pl.BlockSpec(memory_space=pltpu.VMEM)] * len(out_shape),
        scratch_shapes=list(scratch),
        compiler_params=pltpu.CompilerParams(vmem_limit_bytes=mib * 1024 * 1024),
        cost_estimate=pl.CostEstimate(flops=flops, bytes_accessed=size, transcendentals=0),
    )(*args)


def latents_body(
    scal, start, length, raw_mine, raw_other, w_own, w_relay, w_other, mine, other, w_mine
):
    lane = lax.broadcasted_iota(jnp.int32, (NQ, DR), 1)
    low = start[0] + NQ - length[0]
    note = jnp.zeros((NQ, DR), F32)
    for n, v in enumerate((start[0] // NQ, start[0] % NQ, low // NQ, low % NQ)):
        note = jnp.where(lane == n, v.astype(F32), note)
    note = note.astype(BF)

    @pl.when(scal[4] == 1)
    def _():
        w_mine[...] = w_own[...]

    @pl.when(scal[4] == 0)
    def _():
        w_mine[...] = w_relay[...]

    for raw, w, out in ((raw_mine, w_mine, mine), (raw_other, w_other, other)):
        for h in range(HEADS):
            rows = slice(h * NQ, (h + 1) * NQ)
            nope = raw[:, h * (DN + DR) : h * (DN + DR) + DN]
            at = HEADS * (DN + DR) + h * DV
            grad = raw[:, at : at + DV]
            wk = w[:, h * (DN + DV) : h * (DN + DV) + DN]
            wv = w[:, h * (DN + DV) + DN : (h + 1) * (DN + DV)]
            out[rows, :C] = dot(grad, wv, 1, 1).astype(BF)
            out[rows, C : 2 * C] = dot(nope, wk, 1, 1).astype(BF)
            out[rows, 2 * C : C + W] = raw[:, h * (DN + DR) + DN : (h + 1) * (DN + DR)]
            out[rows, C + W :] = note


def join_body(*refs):
    for b in range(NZ):
        refs[NZ][:, b * BLK : (b + 1) * BLK] = refs[b][...]


def scores_body(*refs):
    scal, mine, other = refs[:3]
    keys = refs[3:5]
    e_mine, e_their, kt, stats, s_ref, gp_ref, wide = refs[5:]
    z, y_own = scal[0], scal[1]
    for n in range(2):
        kt[:, n * NZ * BLK : (n + 1) * NZ * BLK] = keys[n][...]
    note = mine[0:16, 2 * C :].astype(F32).astype(jnp.int32)[0:8, :]
    start = note[:, DR : DR + 1] * NQ + note[:, DR + 1 : DR + 2]
    low = note[:, DR + 2 : DR + 3] * NQ + note[:, DR + 3 : DR + 4]
    lane = lax.broadcasted_iota(jnp.int32, (8, BLK), 1)
    sub = lax.broadcasted_iota(jnp.int32, (8, BLK), 0)
    above = lane - low
    ahead = lane - start - sub
    base = []
    for y in (y_own, 3 - y_own):
        for d in OFFSETS:
            base.append(((z + d + NZ) % NZ) * (NY * BLK) + y * BLK)
    for half, qg in ((0, mine), (1, other)):
        rows = slice(half * ROWS, (half + 1) * ROWS)
        q = qg[:, C : C + W]
        g = qg[:, :C]
        for t in range(KEYS // TILE):
            cols = slice(t * TILE, (t + 1) * TILE)
            s_ref[rows, cols] = dot(q, kt[:, cols])
            gp_ref[rows, cols] = dot(g, kt[:C, cols])
    chunk = NQ

    @pl.loop(0, 2 * ROWS // chunk)
    def _(i):
        r0 = pl.multiple_of(i * chunk, chunk)
        here = pl.ds(r0, chunk)
        below = pl.ds(pl.multiple_of(2 * ROWS + r0, chunk), chunk)
        peak = [None] * (chunk // 8)
        for b in range(16):
            cols = slice(b * BLK, (b + 1) * BLK)
            inside = above + base[b] >= 0
            gap = ahead + base[b]
            for k in range(chunk // 8):
                r = pl.ds(pl.multiple_of(r0 + 8 * k, 8), 8)
                ok = inside & (gap <= 8 * k)
                v = jnp.where(ok, s_ref[r, cols] * SCALE, NEG_FILL)
                s_ref[r, cols] = v
                peak[k] = v if peak[k] is None else jnp.maximum(peak[k], v)
        m = jnp.max(jnp.concatenate(peak, axis=0), axis=1, keepdims=True)
        safe = jnp.broadcast_to(jnp.maximum(m, 0.1 * NEG_FILL), (chunk, BLK))
        total = None
        rsum = None
        for b in range(16):
            cols = slice(b * BLK, (b + 1) * BLK)
            e = jnp.exp(s_ref[here, cols] - safe)
            s_ref[here, cols] = e
            p = e * gp_ref[here, cols]
            total = e if total is None else total + e
            rsum = p if rsum is None else rsum + p
        l = jnp.sum(total, axis=1, keepdims=True)
        rd = jnp.sum(rsum, axis=1, keepdims=True) / jnp.where(l > 0.0, l, 1.0)
        rdb = jnp.broadcast_to(rd, (chunk, BLK))
        for b in range(16):
            cols = slice(b * BLK, (b + 1) * BLK)
            out = e_mine if b < 8 else e_their
            oc = slice((b % 8) * BLK, (b % 8 + 1) * BLK)
            e = s_ref[here, cols]
            out[here, oc] = (e * (gp_ref[here, cols] - rdb)).astype(BF)
            out[below, oc] = e.astype(BF)
        col = lax.broadcasted_iota(jnp.int32, (chunk, BLK), 1)
        wide[here, :] = jnp.where(col == 0, m, jnp.where(col == 1, l, rd))

    stats[...] = jnp.transpose(wide[...])[0:8, :]


def key_parts(qq, ee, out):
    for k in range(NZ // 2):
        r = dot(qq[...], ee[:, k * TILE : (k + 1) * TILE], 0, 0)
        for n in range(2):
            out[2 * k + n] = r[:, n * BLK : (n + 1) * BLK].astype(BF)


def add_body(a, b, *outs):
    for k in range(NZ):
        outs[k][...] = (a[k].astype(F32) + b[k].astype(F32)).astype(BF)


def total_body(*refs):
    acc = refs[0][...].astype(F32)
    for ref in refs[1:-1]:
        acc = acc + ref[...].astype(F32)
    refs[-1][...] = acc.astype(BF)


def first_body(st, their, mine, other, ee, qq, ws, out):
    there = jnp.concatenate([their[:, ROWS:], their[:, :ROWS]], axis=1)
    m, l, rd = st[0:1, :], st[1:2, :], st[2:3, :]
    m2, l2, rd2 = there[0:1, :], there[1:2, :], there[2:3, :]
    top = jnp.maximum(m, m2)
    a = jnp.exp(m - top)
    a2 = jnp.exp(m2 - top)
    denom = l * a + l2 * a2
    shift = (rd * l * a + rd2 * l2 * a2) / denom - rd
    w = a / denom
    row = lax.broadcasted_iota(jnp.int32, (BLK, 2 * ROWS), 0)
    ws[...] = jnp.transpose(jnp.where(row == 0, w, shift))
    step = 64
    for half, qg in ((0, mine), (1, other)):

        @pl.loop(0, ROWS // step)
        def _(i):
            r = pl.multiple_of(i * step, step)
            at = pl.multiple_of(half * ROWS + r, step)
            rows = pl.ds(at, step)
            below = pl.ds(pl.multiple_of(at + 2 * ROWS, step), step)
            wv = ws[rows, 0:1]
            dv = ws[rows, 1:2]
            q = qg[pl.ds(r, step), C : C + W].astype(F32)
            g = qg[pl.ds(r, step), :C].astype(F32)
            qs = q * (SCALE * wv)
            qq[rows, :] = qs.astype(BF)
            qd = qs * dv
            qq[below, :C] = (g * wv - qd[:, :C]).astype(BF)
            qq[below, C:] = (-qd[:, C:]).astype(BF)

    key_parts(qq, ee, out)


def parts_body(qq, ee, out):
    key_parts(qq, ee, out)


def query_body(ws, kt, e0, e1, mine, other):
    for half, out in ((0, mine), (1, other)):
        xs = []
        for top in (0, 2 * ROWS):
            rows = slice(top + half * ROWS, top + (half + 1) * ROWS)
            acc = None
            at = 0
            for e in (e0, e1):
                n = e.shape[1]
                r = dot(e[rows, :], kt[:, at : at + n], 1, 1)
                acc = r if acc is None else acc + r
                at += n
            xs.append(acc)
        rows = slice(half * ROWS, (half + 1) * ROWS)
        w = ws[rows, 0:1]
        shift = ws[rows, 1:2]
        out[:, :C] = (w * xs[1][:, :C]).astype(out.dtype)
        out[:, C : C + W] = ((SCALE * w) * (xs[0] - shift * xs[1])).astype(out.dtype)
        out[:, C + W :] = jnp.zeros((ROWS, DR), out.dtype)


def tail_body(scal, came, held, both, w, gq, keep, send, terms):
    home = scal[4].astype(F32)
    for h in range(HEADS):
        rows = slice(h * NQ, (h + 1) * NQ)
        qo = (came[rows, :].astype(F32) + held[rows, :].astype(F32) * home).astype(BF)
        o = qo[:, :C]
        lat = qo[:, C : 2 * C]
        nope = both[:, h * (DN + DR) : h * (DN + DR) + DN]
        at = HEADS * (DN + DR) + h * DV
        grad = both[:, at : at + DV]
        c0 = h * (DN + DV)
        terms[:, c0 : c0 + DN] = dot(lat, nope, 0, 0).astype(BF)
        terms[:, c0 + DN : c0 + DN + DV] = dot(o, grad, 0, 0).astype(BF)
        q0 = h * (DN + DR)
        gq[:, q0 : q0 + DN] = dot(lat, w[:, c0 : c0 + DN]).astype(BF)
        gq[:, q0 + DN : q0 + DN + DR] = qo[:, 2 * C : C + W]
    x, c = scal[2], scal[3]
    n = C // 8
    for k in range(4):
        base = lax.rem(x + k, 4) * (2 * n)
        slot = slice(k * n, (k + 1) * n)
        keep[slot, :] = terms[pl.ds(pl.multiple_of(base + c * n, n), n), :]
        send[slot, :] = terms[pl.ds(pl.multiple_of(base + (1 - c) * n, n), n), :]


def step(queries, grad_out, latent, latent_up, query_start, key_lengths):
    ndev = NZ * NY
    own_q = queries.shape[1]

    zi = lax.axis_index("z")
    yi = lax.axis_index("y")
    ci = lax.axis_index("core")
    home = (yi >> 1) == ci
    y_own = jnp.where(home, yi, 3 - yi)
    scal = jnp.stack([zi, y_own, lax.axis_index("x"), ci, home.astype(jnp.int32)])

    own = swap(latent[0].T)
    both = jnp.concatenate(
        [
            queries.reshape(own_q, ndev, HEADS * (DN + DR)),
            grad_out.reshape(own_q, ndev, HEADS * DV),
        ],
        axis=2,
    )
    both = jnp.moveaxis(both, 1, 0)
    both = lax.all_to_all(both, CTX, 0, 0, tiled=True)
    both = both.reshape(NQ, RAW)
    w_other = in_hbm(turn(latent_up, 1))
    w_relay = in_hbm(relay(w_other))

    near = {0: own}
    for d in (-3, 3, -2, 2, -1, 1):
        near[d] = along_z(own, -d)
    near[4] = along_z(near[3], -1)
    kept = [near[d] for d in OFFSETS]

    raw_mine = turn(both, 0)
    raw_other = turn(both, 1)
    start = swap(query_start)
    length = swap(key_lengths)
    qg_mine, qg_other = call(
        latents_body,
        [vmem((ROWS, WIDE), BF)] * 2,
        (scal, start, length, raw_mine, raw_other, in_hbm(latent_up), w_relay, w_other),
        540_000_000,
        (pltpu.VMEM((C, HEADS * (DN + DV)), BF),),
        smem=3,
        mib=12,
    )
    (mine_side,) = call(join_body, [vmem((W, NZ * BLK), BF)], kept, 1_000_000, mib=6)
    their_side = other_core(mine_side)

    half = vmem((4 * ROWS, NZ * BLK), BF)
    big = pltpu.VMEM((2 * ROWS, KEYS), F32)
    e_mine, e_their, kt, stats = call(
        scores_body,
        [half, half, vmem((W, KEYS), BF), vmem((8, 2 * ROWS), F32)],
        (scal, qg_mine, qg_other, mine_side, their_side),
        2_280_000_000,
        (big, big, pltpu.VMEM((2 * ROWS, BLK), F32)),
        smem=1,
    )
    theirs = pair_y(stats)

    piece = vmem((NZ, W, BLK), BF)
    qq, ws, their_keys = call(
        first_body,
        [vmem((4 * ROWS, W), BF), vmem((2 * ROWS, BLK), F32), piece],
        (stats, theirs, qg_mine, qg_other, e_their),
        1_300_000_000,
    )
    their_keys = other_core(their_keys)
    (mine_keys,) = call(parts_body, [piece], (qq, e_mine), 1_200_000_000, mib=12)
    sums = call(add_body, [vmem((W, BLK), BF)] * NZ, (mine_keys, their_keys), 1_000_000, mib=8)
    sums, ws = lax.optimization_barrier((sums, ws))
    sums = dict(zip(OFFSETS, sums))
    early = along_z(sums[4], -1)
    moved = [sums[0]]
    for d in (3, -2, 2, -1, 1):
        moved.append(along_z(sums[d], d))
    moved.append(along_z((sums[-3].astype(F32) + early.astype(F32)).astype(BF), -3))
    (total,) = call(total_body, [vmem((W, BLK), BF)], moved, 1_000_000, mib=4)
    key_grad = swap(total)
    key_grad = key_grad.astype(F32).T

    mine, other = call(
        query_body,
        [vmem((ROWS, WIDE), BF), vmem((ROWS, WIDE), BF)],
        (ws, kt, e_mine, e_their),
        2_400_000_000,
    )
    passed = relay(mine)
    other = (other.astype(F32) + jnp.where(home, 0.0, passed.astype(F32))).astype(BF)
    came = turn(other, 1)
    wide = HEADS * (DN + DV)
    gq, keep, send = call(
        tail_body,
        [vmem((NQ, HEADS * (DN + DR)), BF)] + [vmem((C // 2, wide), BF)] * 2,
        (scal, came, mine, both, in_hbm(latent_up)),
        200_000_000,
        (pltpu.VMEM((C, wide), BF),),
        smem=1,
        mib=12,
    )
    got = other_core(send)
    n = C // 8
    grad_weights = keep[:n].astype(F32) + got[:n].astype(F32)
    for k in range(1, 4):
        rows = slice(k * n, (k + 1) * n)
        pair = (keep[rows].astype(F32) + got[rows].astype(F32)).astype(BF)
        pair = lax.ppermute(pair, "x", [(i, (i + k) % 4) for i in range(4)])
        grad_weights = grad_weights + pair.astype(F32)
    back = lax.all_to_all(gq.reshape(ndev, own_q, HEADS * (DN + DR)), CTX, 0, 0, tiled=True)
    grad_queries = jnp.moveaxis(back, 0, 1).reshape(1, own_q, -1).astype(F32)
    return (grad_queries, key_grad[None], grad_weights)


def solution(mesh):
    finer = Mesh(mesh.devices.reshape(4, 2, NZ, NY), ("x", "core", "z", "y"))
    in_specs = (
        P(DP, CTX, None),
        P(DP, CTX, None),
        P(DP, CTX, None),
        P(None, CTX),
        P(DP),
        P(DP),
    )
    out_specs = (P(DP, CTX, None), P(DP, CTX, None), P(DP, CTX))
    return jax.shard_map(step, mesh=finer, in_specs=in_specs, out_specs=out_specs, check_vma=False)
```

```python
import math

import jax
import jax.numpy as jnp
from jax import lax
from jax.experimental import pallas as pl
from jax.experimental.pallas import tpu as pltpu
from jax.sharding import Mesh
from jax.sharding import PartitionSpec as P


DN = 128
DR = 64
DV = 128
C = 512
W = C + DR
NZ = 8
NY = 4
HEADS = 4
NQ = 64
ROWS = NQ * HEADS
WIDE = 2 * C + 2 * DR
BLK = 128
DP = ("x", "core")
CTX = ("z", "y")
MSCALE = 0.1 * math.log(40.0) + 1.0
SCALE = MSCALE * MSCALE / math.sqrt(DN + DR)
NEG_FILL = -1e30
BF = jnp.bfloat16
F32 = jnp.float32
OFFSETS = (0, 4, -3, 3, -2, 2, -1, 1)
KEYS = 2 * NZ * BLK
TILE = 256


def turned(flip):
    pairs = []
    for c in range(2):
        for y in range(NY):
            v, w = y >> 1, y & 1
            pairs.append((c * NY + y, v * NY + 2 * c + (w ^ flip)))
    return pairs


def swap_pairs():
    pairs = []
    for c in range(2):
        for y in range(NY):
            home = (y >> 1) == c
            pairs.append((c * NY + y, c * NY + y if home else (1 - c) * NY + 3 - y))
    return pairs


def swap(v):
    return lax.ppermute(v, ("core", "y"), swap_pairs())


def turn(v, flip):
    return lax.ppermute(v, ("core", "y"), turned(flip))


def homeward(v, d):
    pairs = []
    for c in range(2):
        for z in range(NZ):
            for y in range(NY):
                here = (y >> 1) == c
                to = (c, y) if here else (1 - c, 3 - y)
                pairs.append(((c * NZ + z) * NY + y, (to[0] * NZ + (z + d) % NZ) * NY + to[1]))
    return lax.ppermute(v, ("core", "z", "y"), pairs)


def other_core(v):
    return lax.ppermute(v, "core", [(0, 1), (1, 0)])


def pair_y(v):
    return lax.ppermute(v, "y", [(i, i ^ 1) for i in range(NY)])


def along_z(v, step):
    return lax.ppermute(v, "z", [(i, (i + step) % NZ) for i in range(NZ)])


def dot(a, b, da=1, db=0):
    return lax.dot_general(a, b, (((da,), (db,)), ((), ())), preferred_element_type=F32)


def in_hbm(v):
    return pltpu.with_memory_space_constraint(v, pltpu.HBM)


def vmem(shape, dtype):
    return jax.ShapeDtypeStruct(shape, dtype)


def call(body, out_shape, args, flops, scratch=(), smem=0, mib=32):
    specs = [pl.BlockSpec(memory_space=pltpu.SMEM)] * smem
    specs += [pl.BlockSpec(memory_space=pltpu.VMEM)] * (len(args) - smem)
    size = sum(a.size * a.dtype.itemsize for a in args)
    size += sum(o.size * o.dtype.itemsize for o in out_shape)
    return pl.pallas_call(
        body,
        out_shape=out_shape,
        in_specs=specs,
        out_specs=[pl.BlockSpec(memory_space=pltpu.VMEM)] * len(out_shape),
        scratch_shapes=list(scratch),
        compiler_params=pltpu.CompilerParams(vmem_limit_bytes=mib * 1024 * 1024),
        cost_estimate=pl.CostEstimate(flops=flops, bytes_accessed=size, transcendentals=0),
    )(*args)


def latents_body(start, length, both, w, out):
    lane = lax.broadcasted_iota(jnp.int32, (NQ, DR), 1)
    note = jnp.zeros((NQ, DR), F32)
    low = start[0] + NQ - length[0]
    for n, v in enumerate((start[0] // NQ, start[0] % NQ, low // NQ, low % NQ)):
        note = jnp.where(lane == n, v.astype(F32), note)
    note = note.astype(BF)
    for h in range(HEADS):
        rows = slice(h * NQ, (h + 1) * NQ)
        nope = both[:, h * (DN + DR) : h * (DN + DR) + DN]
        rope = both[:, h * (DN + DR) + DN : (h + 1) * (DN + DR)]
        at = HEADS * (DN + DR) + h * DV
        grad = both[:, at : at + DV]
        wk = w[:, h * (DN + DV) : h * (DN + DV) + DN]
        wv = w[:, h * (DN + DV) + DN : (h + 1) * (DN + DV)]
        out[rows, :C] = dot(grad, wv, 1, 1).astype(BF)
        out[rows, C : 2 * C] = dot(nope, wk, 1, 1).astype(BF)
        out[rows, 2 * C : C + W] = rope
        out[rows, C + W :] = note


def join_body(*refs):
    for b in range(NZ):
        refs[NZ][:, b * BLK : (b + 1) * BLK] = refs[b][...]


def scores_body(*refs):
    scal, mine, other = refs[:3]
    keys = refs[3:5]
    e_mine, e_their, kt, stats, s_ref, gp_ref, wide = refs[5:]
    z, y_own = scal[0], scal[1]
    for n in range(2):
        kt[:, n * NZ * BLK : (n + 1) * NZ * BLK] = keys[n][...]
    note = mine[0:16, 2 * C :].astype(F32).astype(jnp.int32)[0:8, :]
    start = note[:, DR : DR + 1] * NQ + note[:, DR + 1 : DR + 2]
    low = note[:, DR + 2 : DR + 3] * NQ + note[:, DR + 3 : DR + 4]
    lane = lax.broadcasted_iota(jnp.int32, (8, BLK), 1)
    sub = lax.broadcasted_iota(jnp.int32, (8, BLK), 0)
    above = lane - low
    ahead = lane - start - sub
    base = []
    for y in (y_own, 3 - y_own):
        for d in OFFSETS:
            base.append(((z + d + NZ) % NZ) * (NY * BLK) + y * BLK)
    for half, qg in ((0, mine), (1, other)):
        rows = slice(half * ROWS, (half + 1) * ROWS)
        q = qg[:, C : C + W]
        g = qg[:, :C]
        for t in range(KEYS // TILE):
            cols = slice(t * TILE, (t + 1) * TILE)
            s_ref[rows, cols] = dot(q, kt[:, cols])
            gp_ref[rows, cols] = dot(g, kt[:C, cols])
    chunk = NQ

    @pl.loop(0, 2 * ROWS // chunk)
    def _(i):
        r0 = pl.multiple_of(i * chunk, chunk)
        here = pl.ds(r0, chunk)
        below = pl.ds(pl.multiple_of(2 * ROWS + r0, chunk), chunk)
        peak = [None] * (chunk // 8)
        for b in range(16):
            cols = slice(b * BLK, (b + 1) * BLK)
            inside = above + base[b] >= 0
            gap = ahead + base[b]
            for k in range(chunk // 8):
                r = pl.ds(pl.multiple_of(r0 + 8 * k, 8), 8)
                ok = inside & (gap <= 8 * k)
                v = jnp.where(ok, s_ref[r, cols] * SCALE, NEG_FILL)
                s_ref[r, cols] = v
                peak[k] = v if peak[k] is None else jnp.maximum(peak[k], v)
        m = jnp.max(jnp.concatenate(peak, axis=0), axis=1, keepdims=True)
        safe = jnp.broadcast_to(jnp.maximum(m, 0.1 * NEG_FILL), (chunk, BLK))
        total = None
        rsum = None
        for b in range(16):
            cols = slice(b * BLK, (b + 1) * BLK)
            e = jnp.exp(s_ref[here, cols] - safe)
            s_ref[here, cols] = e
            p = e * gp_ref[here, cols]
            total = e if total is None else total + e
            rsum = p if rsum is None else rsum + p
        l = jnp.sum(total, axis=1, keepdims=True)
        rd = jnp.sum(rsum, axis=1, keepdims=True) / jnp.where(l > 0.0, l, 1.0)
        rdb = jnp.broadcast_to(rd, (chunk, BLK))
        for b in range(16):
            cols = slice(b * BLK, (b + 1) * BLK)
            out = e_mine if b < 8 else e_their
            oc = slice((b % 8) * BLK, (b % 8 + 1) * BLK)
            e = s_ref[here, cols]
            out[here, oc] = (e * (gp_ref[here, cols] - rdb)).astype(BF)
            out[below, oc] = e.astype(BF)
        col = lax.broadcasted_iota(jnp.int32, (chunk, BLK), 1)
        wide[here, :] = jnp.where(col == 0, m, jnp.where(col == 1, l, rd))

    stats[...] = jnp.transpose(wide[...])[0:8, :]


def key_parts(qq, ee, out):
    for k in range(NZ // 2):
        r = dot(qq[...], ee[:, k * TILE : (k + 1) * TILE], 0, 0)
        for n in range(2):
            out[2 * k + n] = r[:, n * BLK : (n + 1) * BLK].astype(BF)


def add_body(a, b, *outs):
    for k in range(NZ):
        outs[k][...] = (a[k].astype(F32) + b[k].astype(F32)).astype(BF)


def total_body(*refs):
    acc = refs[0][...].astype(F32)
    for k in range(1, NZ):
        acc = acc + refs[k][...].astype(F32)
    refs[NZ][...] = acc.astype(BF)


def row_factors(st, their, ws):
    there = jnp.concatenate([their[:, ROWS:], their[:, :ROWS]], axis=1)
    m, l, rd = st[0:1, :], st[1:2, :], st[2:3, :]
    m2, l2, rd2 = there[0:1, :], there[1:2, :], there[2:3, :]
    top = jnp.maximum(m, m2)
    a = jnp.exp(m - top)
    a2 = jnp.exp(m2 - top)
    denom = l * a + l2 * a2
    shift = (rd * l * a + rd2 * l2 * a2) / denom - rd
    row = lax.broadcasted_iota(jnp.int32, (BLK, 2 * ROWS), 0)
    ws[...] = jnp.transpose(jnp.where(row == 0, a / denom, shift))


def first_body(ws, mine, other, ee, qq, out):
    step = 64
    for half, qg in ((0, mine), (1, other)):

        @pl.loop(0, ROWS // step)
        def _(i):
            r = pl.multiple_of(i * step, step)
            at = pl.multiple_of(half * ROWS + r, step)
            rows = pl.ds(at, step)
            below = pl.ds(pl.multiple_of(at + 2 * ROWS, step), step)
            wv = ws[rows, 0:1]
            dv = ws[rows, 1:2]
            q = qg[pl.ds(r, step), C : C + W].astype(F32)
            g = qg[pl.ds(r, step), :C].astype(F32)
            qs = q * (SCALE * wv)
            qq[rows, :] = qs.astype(BF)
            qd = qs * dv
            qq[below, :C] = (g * wv - qd[:, :C]).astype(BF)
            qq[below, C:] = (-qd[:, C:]).astype(BF)

    key_parts(qq, ee, out)


def parts_body(qq, ee, out):
    key_parts(qq, ee, out)


def query_body(st, their, kt, e0, e1, mine, other, ws):
    row_factors(st, their, ws)
    for half, out in ((0, mine), (1, other)):
        xs = []
        for top in (0, 2 * ROWS):
            rows = slice(top + half * ROWS, top + (half + 1) * ROWS)
            acc = None
            at = 0
            for e in (e0, e1):
                n = e.shape[1]
                r = dot(e[rows, :], kt[:, at : at + n], 1, 1)
                acc = r if acc is None else acc + r
                at += n
            xs.append(acc)
        rows = slice(half * ROWS, (half + 1) * ROWS)
        w = ws[rows, 0:1]
        shift = ws[rows, 1:2]
        out[:, :C] = (w * xs[1][:, :C]).astype(out.dtype)
        out[:, C : C + W] = ((SCALE * w) * (xs[0] - shift * xs[1])).astype(out.dtype)
        out[:, C + W :] = jnp.zeros((ROWS, DR), out.dtype)


def tail_body(scal, qo, both, w, gq, keep, send, terms):
    for h in range(HEADS):
        rows = slice(h * NQ, (h + 1) * NQ)
        o = qo[rows, :C]
        lat = qo[rows, C : 2 * C]
        nope = both[:, h * (DN + DR) : h * (DN + DR) + DN]
        at = HEADS * (DN + DR) + h * DV
        grad = both[:, at : at + DV]
        c0 = h * (DN + DV)
        terms[:, c0 : c0 + DN] = dot(lat, nope, 0, 0).astype(BF)
        terms[:, c0 + DN : c0 + DN + DV] = dot(o, grad, 0, 0).astype(BF)
        q0 = h * (DN + DR)
        gq[:, q0 : q0 + DN] = dot(lat, w[:, c0 : c0 + DN]).astype(BF)
        gq[:, q0 + DN : q0 + DN + DR] = qo[rows, 2 * C : C + W]
    x, c = scal[2], scal[3]
    n = C // 8
    for k in range(4):
        base = lax.rem(x + k, 4) * (2 * n)
        slot = slice(k * n, (k + 1) * n)
        keep[slot, :] = terms[pl.ds(pl.multiple_of(base + c * n, n), n), :]
        send[slot, :] = terms[pl.ds(pl.multiple_of(base + (1 - c) * n, n), n), :]


def step(queries, grad_out, latent, latent_up, query_start, key_lengths):
    ndev = NZ * NY
    own_q = queries.shape[1]

    own = swap(latent[0].T)
    both = jnp.concatenate(
        [
            queries.reshape(own_q, ndev, HEADS * (DN + DR)),
            grad_out.reshape(own_q, ndev, HEADS * DV),
        ],
        axis=2,
    )
    both = jnp.moveaxis(both, 1, 0)
    both = lax.all_to_all(both, CTX, 0, 0, tiled=True)
    both = both.reshape(NQ, HEADS * (DN + DR + DV))

    kept = [own] + [along_z(own, -d) for d in OFFSETS[1:]]

    (qg,) = call(
        latents_body,
        [vmem((ROWS, WIDE), BF)],
        (query_start, key_lengths, both, in_hbm(latent_up)),
        270_000_000,
        smem=2,
        mib=12,
    )
    qg_mine = turn(qg, 0)
    qg_other = turn(qg, 1)
    (mine_side,) = call(join_body, [vmem((W, NZ * BLK), BF)], kept, 1_000_000, mib=6)
    their_side = other_core(mine_side)

    zi = lax.axis_index("z")
    yi = lax.axis_index("y")
    ci = lax.axis_index("core")
    y_own = jnp.where((yi >> 1) == ci, yi, 3 - yi)
    scal = jnp.stack([zi, y_own, lax.axis_index("x"), ci]).astype(jnp.int32)
    half = vmem((4 * ROWS, NZ * BLK), BF)
    big = pltpu.VMEM((2 * ROWS, KEYS), F32)
    e_mine, e_their, kt, stats = call(
        scores_body,
        [half, half, vmem((W, KEYS), BF), vmem((8, 2 * ROWS), F32)],
        (scal, qg_mine, qg_other, mine_side, their_side),
        2_280_000_000,
        (big, big, pltpu.VMEM((2 * ROWS, BLK), F32)),
        smem=1,
    )
    theirs = pair_y(stats)

    mine, other, ws = call(
        query_body,
        [vmem((ROWS, WIDE), BF), vmem((ROWS, WIDE), BF), vmem((2 * ROWS, BLK), F32)],
        (stats, theirs, kt, e_mine, e_their),
        2_400_000_000,
    )
    mine, other = turn(mine, 0), turn(other, 1)
    piece = vmem((NZ, W, BLK), BF)
    qq, their_keys = call(
        first_body,
        [vmem((4 * ROWS, W), BF), piece],
        (ws, qg_mine, qg_other, e_their),
        1_300_000_000,
    )
    their_keys = other_core(their_keys)
    (mine_keys,) = call(parts_body, [piece], (qq, e_mine), 1_200_000_000)
    sums = call(add_body, [vmem((W, BLK), BF)] * NZ, (mine_keys, their_keys), 1_000_000, mib=8)
    moved = []
    for n in (1, 2, 3, 4, 5, 0, 6, 7):
        moved.append(homeward(sums[n], OFFSETS[n]))
    (total,) = call(total_body, [vmem((W, BLK), BF)], moved, 1_000_000, mib=4)
    key_grad = total.astype(F32).T

    qo = (mine.astype(F32) + other.astype(F32)).astype(BF)
    wide = HEADS * (DN + DV)
    gq, keep, send = call(
        tail_body,
        [vmem((NQ, HEADS * (DN + DR)), BF)] + [vmem((C // 2, wide), BF)] * 2,
        (scal, qo, both, in_hbm(latent_up)),
        200_000_000,
        (pltpu.VMEM((C, wide), BF),),
        smem=1,
        mib=12,
    )
    got = other_core(send)
    n = C // 8
    grad_weights = keep[:n].astype(F32) + got[:n].astype(F32)
    for k in range(1, 4):
        rows = slice(k * n, (k + 1) * n)
        pair = (keep[rows].astype(F32) + got[rows].astype(F32)).astype(BF)
        pair = lax.ppermute(pair, "x", [(i, (i + k) % 4) for i in range(4)])
        grad_weights = grad_weights + pair.astype(F32)
    back = lax.all_to_all(gq.reshape(ndev, own_q, HEADS * (DN + DR)), CTX, 0, 0, tiled=True)
    grad_queries = jnp.moveaxis(back, 0, 1).reshape(1, own_q, -1).astype(F32)
    return (grad_queries, key_grad[None], grad_weights)


def solution(mesh):
    finer = Mesh(mesh.devices.reshape(4, 2, NZ, NY), ("x", "core", "z", "y"))
    in_specs = (
        P(DP, CTX, None),
        P(DP, CTX, None),
        P(DP, CTX, None),
        P(None, CTX),
        P(DP),
        P(DP),
    )
    out_specs = (P(DP, CTX, None), P(DP, CTX, None), P(DP, CTX))
    return jax.shard_map(step, mesh=finer, in_specs=in_specs, out_specs=out_specs, check_vma=False)
```

```python
import math

import jax
import jax.numpy as jnp
from jax import lax
from jax.experimental import pallas as pl
from jax.experimental.pallas import tpu as pltpu
from jax.sharding import Mesh
from jax.sharding import PartitionSpec as P


DN = 128
DR = 64
DV = 128
C = 512
W = C + DR
NZ = 8
NY = 4
HEADS = 4
NQ = 64
ROWS = NQ * HEADS
WIDE = 2 * C + 2 * DR
BLK = 128
DP = ("x", "core")
CTX = ("z", "y")
MSCALE = 0.1 * math.log(40.0) + 1.0
SCALE = MSCALE * MSCALE / math.sqrt(DN + DR)
NEG_FILL = -1e30
BF = jnp.bfloat16
F32 = jnp.float32
OFFSETS = (0, 4, -3, 3, -2, 2, -1, 1)
KEYS = 2 * NZ * BLK
TILE = 256


def turned(flip):
    pairs = []
    for c in range(2):
        for y in range(NY):
            v, w = y >> 1, y & 1
            pairs.append((c * NY + y, v * NY + 2 * c + (w ^ flip)))
    return pairs


def turn(v, flip):
    return lax.ppermute(v, ("core", "y"), turned(flip))


def homeward(v, d):
    pairs = []
    for c in range(2):
        for z in range(NZ):
            for y in range(NY):
                here = (y >> 1) == c
                to = (c, y) if here else (1 - c, 3 - y)
                pairs.append(((c * NZ + z) * NY + y, (to[0] * NZ + (z + d) % NZ) * NY + to[1]))
    return lax.ppermute(v, ("core", "z", "y"), pairs)


def other_core(v):
    return lax.ppermute(v, "core", [(0, 1), (1, 0)])


def pair_y(v):
    return lax.ppermute(v, "y", [(i, i ^ 1) for i in range(NY)])


def along_z(v, step):
    return lax.ppermute(v, "z", [(i, (i + step) % NZ) for i in range(NZ)])


def dot(a, b, da=1, db=0):
    return lax.dot_general(a, b, (((da,), (db,)), ((), ())), preferred_element_type=F32)


def in_hbm(v):
    return pltpu.with_memory_space_constraint(v, pltpu.HBM)


def vmem(shape, dtype):
    return jax.ShapeDtypeStruct(shape, dtype)


def call(body, out_shape, args, flops, scratch=(), smem=0, mib=32):
    specs = [pl.BlockSpec(memory_space=pltpu.SMEM)] * smem
    specs += [pl.BlockSpec(memory_space=pltpu.VMEM)] * (len(args) - smem)
    size = sum(a.size * a.dtype.itemsize for a in args)
    size += sum(o.size * o.dtype.itemsize for o in out_shape)
    return pl.pallas_call(
        body,
        out_shape=out_shape,
        in_specs=specs,
        out_specs=[pl.BlockSpec(memory_space=pltpu.VMEM)] * len(out_shape),
        scratch_shapes=list(scratch),
        compiler_params=pltpu.CompilerParams(vmem_limit_bytes=mib * 1024 * 1024),
        cost_estimate=pl.CostEstimate(flops=flops, bytes_accessed=size, transcendentals=0),
    )(*args)


def latents_body(start, length, both, w, out):
    lane = lax.broadcasted_iota(jnp.int32, (NQ, DR), 1)
    note = jnp.zeros((NQ, DR), F32)
    low = start[0] + NQ - length[0]
    for n, v in enumerate((start[0] // NQ, start[0] % NQ, low // NQ, low % NQ)):
        note = jnp.where(lane == n, v.astype(F32), note)
    note = note.astype(BF)
    for h in range(HEADS):
        rows = slice(h * NQ, (h + 1) * NQ)
        nope = both[:, h * (DN + DR) : h * (DN + DR) + DN]
        rope = both[:, h * (DN + DR) + DN : (h + 1) * (DN + DR)]
        at = HEADS * (DN + DR) + h * DV
        grad = both[:, at : at + DV]
        wk = w[:, h * (DN + DV) : h * (DN + DV) + DN]
        wv = w[:, h * (DN + DV) + DN : (h + 1) * (DN + DV)]
        out[rows, :C] = dot(grad, wv, 1, 1).astype(BF)
        out[rows, C : 2 * C] = dot(nope, wk, 1, 1).astype(BF)
        out[rows, 2 * C : C + W] = rope
        out[rows, C + W :] = note


def join_body(*refs):
    for b in range(NZ):
        refs[NZ][:, b * BLK : (b + 1) * BLK] = refs[b][...]


def scores_body(*refs):
    scal, mine, other = refs[:3]
    keys = refs[3:5]
    e_mine, e_their, kt, stats, s_ref, gp_ref, wide = refs[5:]
    z, y_own = scal[0], scal[1]
    for n in range(2):
        kt[:, n * NZ * BLK : (n + 1) * NZ * BLK] = keys[n][...]
    note = mine[0:16, 2 * C :].astype(F32).astype(jnp.int32)[0:8, :]
    start = note[:, DR : DR + 1] * NQ + note[:, DR + 1 : DR + 2]
    low = note[:, DR + 2 : DR + 3] * NQ + note[:, DR + 3 : DR + 4]
    lane = lax.broadcasted_iota(jnp.int32, (8, BLK), 1)
    sub = lax.broadcasted_iota(jnp.int32, (8, BLK), 0)
    above = lane - low
    ahead = lane - start - sub
    base = []
    for y in (y_own, 3 - y_own):
        for d in OFFSETS:
            base.append(((z + d + NZ) % NZ) * (NY * BLK) + y * BLK)
    for half, qg in ((0, mine), (1, other)):
        rows = slice(half * ROWS, (half + 1) * ROWS)
        q = qg[:, C : C + W]
        g = qg[:, :C]
        for t in range(KEYS // TILE):
            cols = slice(t * TILE, (t + 1) * TILE)
            s_ref[rows, cols] = dot(q, kt[:, cols])
            gp_ref[rows, cols] = dot(g, kt[:C, cols])
    chunk = NQ

    @pl.loop(0, 2 * ROWS // chunk)
    def _(i):
        r0 = pl.multiple_of(i * chunk, chunk)
        here = pl.ds(r0, chunk)
        below = pl.ds(pl.multiple_of(2 * ROWS + r0, chunk), chunk)
        peak = [None] * (chunk // 8)
        for b in range(16):
            cols = slice(b * BLK, (b + 1) * BLK)
            inside = above + base[b] >= 0
            gap = ahead + base[b]
            for k in range(chunk // 8):
                r = pl.ds(pl.multiple_of(r0 + 8 * k, 8), 8)
                ok = inside & (gap <= 8 * k)
                v = jnp.where(ok, s_ref[r, cols] * SCALE, NEG_FILL)
                s_ref[r, cols] = v
                peak[k] = v if peak[k] is None else jnp.maximum(peak[k], v)
        m = jnp.max(jnp.concatenate(peak, axis=0), axis=1, keepdims=True)
        safe = jnp.broadcast_to(jnp.maximum(m, 0.1 * NEG_FILL), (chunk, BLK))
        total = None
        rsum = None
        for b in range(16):
            cols = slice(b * BLK, (b + 1) * BLK)
            e = jnp.exp(s_ref[here, cols] - safe)
            s_ref[here, cols] = e
            p = e * gp_ref[here, cols]
            total = e if total is None else total + e
            rsum = p if rsum is None else rsum + p
        l = jnp.sum(total, axis=1, keepdims=True)
        rd = jnp.sum(rsum, axis=1, keepdims=True) / jnp.where(l > 0.0, l, 1.0)
        rdb = jnp.broadcast_to(rd, (chunk, BLK))
        for b in range(16):
            cols = slice(b * BLK, (b + 1) * BLK)
            out = e_mine if b < 8 else e_their
            oc = slice((b % 8) * BLK, (b % 8 + 1) * BLK)
            e = s_ref[here, cols]
            out[here, oc] = (e * (gp_ref[here, cols] - rdb)).astype(BF)
            out[below, oc] = e.astype(BF)
        col = lax.broadcasted_iota(jnp.int32, (chunk, BLK), 1)
        wide[here, :] = jnp.where(col == 0, m, jnp.where(col == 1, l, rd))

    stats[...] = jnp.transpose(wide[...])[0:8, :]


def key_parts(qq, ee, out):
    for k in range(NZ // 2):
        r = dot(qq[...], ee[:, k * TILE : (k + 1) * TILE], 0, 0)
        for n in range(2):
            out[2 * k + n] = r[:, n * BLK : (n + 1) * BLK].astype(BF)


def add_body(a, b, *outs):
    for k in range(NZ):
        outs[k][...] = (a[k].astype(F32) + b[k].astype(F32)).astype(BF)


def row_factors(st, their, ws):
    there = jnp.concatenate([their[:, ROWS:], their[:, :ROWS]], axis=1)
    m, l, rd = st[0:1, :], st[1:2, :], st[2:3, :]
    m2, l2, rd2 = there[0:1, :], there[1:2, :], there[2:3, :]
    top = jnp.maximum(m, m2)
    a = jnp.exp(m - top)
    a2 = jnp.exp(m2 - top)
    denom = l * a + l2 * a2
    shift = (rd * l * a + rd2 * l2 * a2) / denom - rd
    row = lax.broadcasted_iota(jnp.int32, (BLK, 2 * ROWS), 0)
    ws[...] = jnp.transpose(jnp.where(row == 0, a / denom, shift))


def first_body(ws, mine, other, ee, qq, out):
    step = 64
    for half, qg in ((0, mine), (1, other)):

        @pl.loop(0, ROWS // step)
        def _(i):
            r = pl.multiple_of(i * step, step)
            at = pl.multiple_of(half * ROWS + r, step)
            rows = pl.ds(at, step)
            below = pl.ds(pl.multiple_of(at + 2 * ROWS, step), step)
            wv = ws[rows, 0:1]
            dv = ws[rows, 1:2]
            q = qg[pl.ds(r, step), C : C + W].astype(F32)
            g = qg[pl.ds(r, step), :C].astype(F32)
            qs = q * (SCALE * wv)
            qq[rows, :] = qs.astype(BF)
            qd = qs * dv
            qq[below, :C] = (g * wv - qd[:, :C]).astype(BF)
            qq[below, C:] = (-qd[:, C:]).astype(BF)

    key_parts(qq, ee, out)


def parts_body(qq, ee, out):
    key_parts(qq, ee, out)


def query_body(st, their, kt, e0, e1, mine, other, ws):
    row_factors(st, their, ws)
    for half, out in ((0, mine), (1, other)):
        xs = []
        for top in (0, 2 * ROWS):
            rows = slice(top + half * ROWS, top + (half + 1) * ROWS)
            acc = None
            at = 0
            for e in (e0, e1):
                n = e.shape[1]
                r = dot(e[rows, :], kt[:, at : at + n], 1, 1)
                acc = r if acc is None else acc + r
                at += n
            xs.append(acc)
        rows = slice(half * ROWS, (half + 1) * ROWS)
        w = ws[rows, 0:1]
        shift = ws[rows, 1:2]
        out[:, :C] = (w * xs[1][:, :C]).astype(out.dtype)
        out[:, C : C + W] = ((SCALE * w) * (xs[0] - shift * xs[1])).astype(out.dtype)
        out[:, C + W :] = jnp.zeros((ROWS, DR), out.dtype)


def tail_body(scal, qo, both, w, gq, keep, send, terms):
    for h in range(HEADS):
        rows = slice(h * NQ, (h + 1) * NQ)
        o = qo[rows, :C]
        lat = qo[rows, C : 2 * C]
        nope = both[:, h * (DN + DR) : h * (DN + DR) + DN]
        at = HEADS * (DN + DR) + h * DV
        grad = both[:, at : at + DV]
        c0 = h * (DN + DV)
        terms[:, c0 : c0 + DN] = dot(lat, nope, 0, 0).astype(BF)
        terms[:, c0 + DN : c0 + DN + DV] = dot(o, grad, 0, 0).astype(BF)
        q0 = h * (DN + DR)
        gq[:, q0 : q0 + DN] = dot(lat, w[:, c0 : c0 + DN]).astype(BF)
        gq[:, q0 + DN : q0 + DN + DR] = qo[rows, 2 * C : C + W]
    x, c = scal[2], scal[3]
    n = C // 8
    for k in range(4):
        base = lax.rem(x + k, 4) * (2 * n)
        slot = slice(k * n, (k + 1) * n)
        keep[slot, :] = terms[pl.ds(pl.multiple_of(base + c * n, n), n), :]
        send[slot, :] = terms[pl.ds(pl.multiple_of(base + (1 - c) * n, n), n), :]


def plus(a, b):
    return (a.astype(F32) + b.astype(F32)).astype(BF)


def step(queries, grad_out, latent, latent_up, query_start, key_lengths):
    ndev = NZ * NY
    own_q = queries.shape[1]

    own = latent[0].T
    both = jnp.concatenate(
        [
            queries.reshape(own_q, ndev, HEADS * (DN + DR)),
            grad_out.reshape(own_q, ndev, HEADS * DV),
        ],
        axis=2,
    )
    both = jnp.moveaxis(both, 1, 0)
    both = lax.all_to_all(both, CTX, 0, 0, tiled=True)
    both = both.reshape(NQ, HEADS * (DN + DR + DV))

    near = {0: homeward(own, 0)}
    near[-1], near[1] = homeward(own, 1), homeward(own, -1)
    for j in (2, 3):
        near[-j] = along_z(near[1 - j], 1)
        near[j] = along_z(near[j - 1], -1)
    near[4] = along_z(near[-3], 1)
    kept = [near[d] for d in OFFSETS]

    (qg,) = call(
        latents_body,
        [vmem((ROWS, WIDE), BF)],
        (query_start, key_lengths, both, in_hbm(latent_up)),
        270_000_000,
        smem=2,
        mib=12,
    )
    qg_mine = turn(qg, 0)
    qg_other = turn(qg, 1)
    (mine_side,) = call(join_body, [vmem((W, NZ * BLK), BF)], kept, 1_000_000, mib=6)
    their_side = other_core(mine_side)

    zi = lax.axis_index("z")
    yi = lax.axis_index("y")
    ci = lax.axis_index("core")
    y_own = jnp.where((yi >> 1) == ci, yi, 3 - yi)
    scal = jnp.stack([zi, y_own, lax.axis_index("x"), ci]).astype(jnp.int32)
    half = vmem((4 * ROWS, NZ * BLK), BF)
    big = pltpu.VMEM((2 * ROWS, KEYS), F32)
    e_mine, e_their, kt, stats = call(
        scores_body,
        [half, half, vmem((W, KEYS), BF), vmem((8, 2 * ROWS), F32)],
        (scal, qg_mine, qg_other, mine_side, their_side),
        2_280_000_000,
        (big, big, pltpu.VMEM((2 * ROWS, BLK), F32)),
        smem=1,
    )
    theirs = pair_y(stats)

    mine, other, ws = call(
        query_body,
        [vmem((ROWS, WIDE), BF), vmem((ROWS, WIDE), BF), vmem((2 * ROWS, BLK), F32)],
        (stats, theirs, kt, e_mine, e_their),
        2_400_000_000,
    )
    mine, other = turn(mine, 0), turn(other, 1)
    piece = vmem((NZ, W, BLK), BF)
    qq, their_keys = call(
        first_body,
        [vmem((4 * ROWS, W), BF), piece],
        (ws, qg_mine, qg_other, e_their),
        1_300_000_000,
    )
    their_keys = other_core(their_keys)
    (mine_keys,) = call(parts_body, [piece], (qq, e_mine), 1_200_000_000)
    sums = call(add_body, [vmem((W, BLK), BF)] * NZ, (mine_keys, their_keys), 1_000_000, mib=8)
    part = dict(zip(OFFSETS, sums))
    f = along_z(part[4], 1)
    b = along_z(part[-3], -1)
    stay = homeward(part[0], 0)
    f = plus(part[3], f)
    b = plus(part[-2], b)
    f = along_z(f, 1)
    b = along_z(b, -1)
    f = plus(part[2], f)
    b = plus(part[-1], b)
    f = along_z(f, 1)
    b = homeward(b, -1)
    f = plus(part[1], f)
    f = homeward(f, 1)
    key_grad = (stay.astype(F32) + b.astype(F32) + f.astype(F32)).T

    qo = (mine.astype(F32) + other.astype(F32)).astype(BF)
    wide = HEADS * (DN + DV)
    gq, keep, send = call(
        tail_body,
        [vmem((NQ, HEADS * (DN + DR)), BF)] + [vmem((C // 2, wide), BF)] * 2,
        (scal, qo, both, latent_up),
        200_000_000,
        (pltpu.VMEM((C, wide), BF),),
        smem=1,
        mib=12,
    )
    got = other_core(send)
    n = C // 8
    grad_weights = keep[:n].astype(F32) + got[:n].astype(F32)
    for k in range(1, 4):
        rows = slice(k * n, (k + 1) * n)
        pair = (keep[rows].astype(F32) + got[rows].astype(F32)).astype(BF)
        pair = lax.ppermute(pair, "x", [(i, (i + k) % 4) for i in range(4)])
        grad_weights = grad_weights + pair.astype(F32)
    back = lax.all_to_all(gq.reshape(ndev, own_q, HEADS * (DN + DR)), CTX, 0, 0, tiled=True)
    grad_queries = jnp.moveaxis(back, 0, 1).reshape(1, own_q, -1).astype(F32)
    return (grad_queries, key_grad[None], grad_weights)


def solution(mesh):
    finer = Mesh(mesh.devices.reshape(4, 2, NZ, NY), ("x", "core", "z", "y"))
    in_specs = (
        P(DP, CTX, None),
        P(DP, CTX, None),
        P(DP, CTX, None),
        P(None, CTX),
        P(DP),
        P(DP),
    )
    out_specs = (P(DP, CTX, None), P(DP, CTX, None), P(DP, CTX))
    return jax.shard_map(step, mesh=finer, in_specs=in_specs, out_specs=out_specs, check_vma=False)
```

```python
import math

import jax
import jax.numpy as jnp
from jax import lax
from jax.experimental import pallas as pl
from jax.experimental.pallas import tpu as pltpu
from jax.sharding import Mesh
from jax.sharding import PartitionSpec as P


DN = 128
DR = 64
DV = 128
C = 512
W = C + DR
NZ = 8
NY = 4
HEADS = 4
NQ = 64
ROWS = NQ * HEADS
WIDE = 2 * C + 2 * DR
BLK = 128
DP = ("x", "core")
CTX = ("z", "y")
MSCALE = 0.1 * math.log(40.0) + 1.0
SCALE = MSCALE * MSCALE / math.sqrt(DN + DR)
NEG_FILL = -1e30
BF = jnp.bfloat16
F32 = jnp.float32
OFFSETS = (0, 4, -3, 3, -2, 2, -1, 1)
KEYS = 2 * NZ * BLK
TILE = 256


def turned(flip):
    pairs = []
    for c in range(2):
        for y in range(NY):
            v, w = y >> 1, y & 1
            pairs.append((c * NY + y, v * NY + 2 * c + (w ^ flip)))
    return pairs


def turn(v, flip):
    return lax.ppermute(v, ("core", "y"), turned(flip))


def homeward(v, d):
    pairs = []
    for c in range(2):
        for z in range(NZ):
            for y in range(NY):
                here = (y >> 1) == c
                to = (c, y) if here else (1 - c, 3 - y)
                pairs.append(((c * NZ + z) * NY + y, (to[0] * NZ + (z + d) % NZ) * NY + to[1]))
    return lax.ppermute(v, ("core", "z", "y"), pairs)


def other_core(v):
    return lax.ppermute(v, "core", [(0, 1), (1, 0)])


def pair_y(v):
    return lax.ppermute(v, "y", [(i, i ^ 1) for i in range(NY)])


def along_z(v, step):
    return lax.ppermute(v, "z", [(i, (i + step) % NZ) for i in range(NZ)])


def dot(a, b, da=1, db=0):
    return lax.dot_general(a, b, (((da,), (db,)), ((), ())), preferred_element_type=F32)


def in_hbm(v):
    return pltpu.with_memory_space_constraint(v, pltpu.HBM)


def vmem(shape, dtype):
    return jax.ShapeDtypeStruct(shape, dtype)


def call(body, out_shape, args, flops, scratch=(), smem=0, mib=32):
    specs = [pl.BlockSpec(memory_space=pltpu.SMEM)] * smem
    specs += [pl.BlockSpec(memory_space=pltpu.VMEM)] * (len(args) - smem)
    size = sum(a.size * a.dtype.itemsize for a in args)
    size += sum(o.size * o.dtype.itemsize for o in out_shape)
    return pl.pallas_call(
        body,
        out_shape=out_shape,
        in_specs=specs,
        out_specs=[pl.BlockSpec(memory_space=pltpu.VMEM)] * len(out_shape),
        scratch_shapes=list(scratch),
        compiler_params=pltpu.CompilerParams(vmem_limit_bytes=mib * 1024 * 1024),
        cost_estimate=pl.CostEstimate(flops=flops, bytes_accessed=size, transcendentals=0),
    )(*args)


def latents_body(start, length, both, w, out):
    lane = lax.broadcasted_iota(jnp.int32, (NQ, DR), 1)
    note = jnp.zeros((NQ, DR), F32)
    low = start[0] + NQ - length[0]
    for n, v in enumerate((start[0] // NQ, start[0] % NQ, low // NQ, low % NQ)):
        note = jnp.where(lane == n, v.astype(F32), note)
    note = note.astype(BF)
    for h in range(HEADS):
        rows = slice(h * NQ, (h + 1) * NQ)
        nope = both[:, h * (DN + DR) : h * (DN + DR) + DN]
        rope = both[:, h * (DN + DR) + DN : (h + 1) * (DN + DR)]
        at = HEADS * (DN + DR) + h * DV
        grad = both[:, at : at + DV]
        wk = w[:, h * (DN + DV) : h * (DN + DV) + DN]
        wv = w[:, h * (DN + DV) + DN : (h + 1) * (DN + DV)]
        out[rows, :C] = dot(grad, wv, 1, 1).astype(BF)
        out[rows, C : 2 * C] = dot(nope, wk, 1, 1).astype(BF)
        out[rows, 2 * C : C + W] = rope
        out[rows, C + W :] = note


def join_body(*refs):
    for b in range(NZ):
        refs[NZ][:, b * BLK : (b + 1) * BLK] = refs[b][...]


def scores_body(*refs):
    scal, mine, other = refs[:3]
    keys = refs[3:5]
    e_mine, e_their, kt, stats, s_ref, gp_ref, wide = refs[5:]
    z, y_own = scal[0], scal[1]
    for n in range(2):
        kt[:, n * NZ * BLK : (n + 1) * NZ * BLK] = keys[n][...]
    note = mine[0:16, 2 * C :].astype(F32).astype(jnp.int32)[0:8, :]
    start = note[:, DR : DR + 1] * NQ + note[:, DR + 1 : DR + 2]
    low = note[:, DR + 2 : DR + 3] * NQ + note[:, DR + 3 : DR + 4]
    lane = lax.broadcasted_iota(jnp.int32, (8, BLK), 1)
    sub = lax.broadcasted_iota(jnp.int32, (8, BLK), 0)
    above = lane - low
    ahead = lane - start - sub
    base = []
    for y in (y_own, 3 - y_own):
        for d in OFFSETS:
            base.append(((z + d + NZ) % NZ) * (NY * BLK) + y * BLK)
    for half, qg in ((0, mine), (1, other)):
        rows = slice(half * ROWS, (half + 1) * ROWS)
        q = qg[:, C : C + W]
        g = qg[:, :C]
        for t in range(KEYS // TILE):
            cols = slice(t * TILE, (t + 1) * TILE)
            raw = dot(q, kt[:, cols])
            gp_ref[rows, cols] = dot(g, kt[:C, cols])
            inside = [above + base[2 * t + n] >= 0 for n in range(2)]
            gap = [ahead + base[2 * t + n] for n in range(2)]
            for j in range(NQ // 8):
                ok = [inside[n] & (gap[n] <= 8 * j) for n in range(2)]
                for h in range(HEADS):
                    r = slice(h * NQ + 8 * j, h * NQ + 8 * j + 8)
                    at = slice(half * ROWS + r.start, half * ROWS + r.stop)
                    v = [
                        jnp.where(ok[n], raw[r, n * BLK : (n + 1) * BLK], NEG_FILL)
                        for n in range(2)
                    ]
                    for n in range(2):
                        b = 2 * t + n
                        s_ref[at, b * BLK : (b + 1) * BLK] = v[n]
                    top = jnp.maximum(v[0], v[1])
                    wide[at, :] = top if t == 0 else jnp.maximum(wide[at, :], top)
    chunk = NQ

    @pl.loop(0, 2 * ROWS // chunk)
    def _(i):
        r0 = pl.multiple_of(i * chunk, chunk)
        here = pl.ds(r0, chunk)
        below = pl.ds(pl.multiple_of(2 * ROWS + r0, chunk), chunk)
        m = jnp.max(wide[here, :], axis=1, keepdims=True)
        safe = jnp.broadcast_to(jnp.maximum(m, 0.1 * NEG_FILL), (chunk, BLK))
        total = None
        rsum = None
        for b in range(16):
            cols = slice(b * BLK, (b + 1) * BLK)
            e = jnp.exp2((s_ref[here, cols] - safe) * (SCALE * math.log2(math.e)))
            s_ref[here, cols] = e
            p = e * gp_ref[here, cols]
            total = e if total is None else total + e
            rsum = p if rsum is None else rsum + p
        l = jnp.sum(total, axis=1, keepdims=True)
        rd = jnp.sum(rsum, axis=1, keepdims=True) / jnp.where(l > 0.0, l, 1.0)
        rdb = jnp.broadcast_to(rd, (chunk, BLK))
        for b in range(16):
            cols = slice(b * BLK, (b + 1) * BLK)
            out = e_mine if b < 8 else e_their
            oc = slice((b % 8) * BLK, (b % 8 + 1) * BLK)
            e = s_ref[here, cols]
            out[here, oc] = (e * (gp_ref[here, cols] - rdb)).astype(BF)
            out[below, oc] = e.astype(BF)
        col = lax.broadcasted_iota(jnp.int32, (chunk, BLK), 1)
        wide[here, :] = jnp.where(col == 0, m * SCALE, jnp.where(col == 1, l, rd))

    stats[...] = jnp.transpose(wide[...])[0:8, :]


def key_parts(qq, ee, out):
    for k in range(NZ // 2):
        r = dot(qq[...], ee[:, k * TILE : (k + 1) * TILE], 0, 0)
        for n in range(2):
            out[2 * k + n] = r[:, n * BLK : (n + 1) * BLK].astype(BF)


def add_body(a, b, *outs):
    for k in range(NZ):
        outs[k][...] = (a[k].astype(F32) + b[k].astype(F32)).astype(BF)


def row_factors(st, their, ws):
    there = jnp.concatenate([their[:, ROWS:], their[:, :ROWS]], axis=1)
    m, l, rd = st[0:1, :], st[1:2, :], st[2:3, :]
    m2, l2, rd2 = there[0:1, :], there[1:2, :], there[2:3, :]
    top = jnp.maximum(m, m2)
    a = jnp.exp(m - top)
    a2 = jnp.exp(m2 - top)
    denom = l * a + l2 * a2
    shift = (rd * l * a + rd2 * l2 * a2) / denom - rd
    row = lax.broadcasted_iota(jnp.int32, (BLK, 2 * ROWS), 0)
    ws[...] = jnp.transpose(jnp.where(row == 0, a / denom, shift))


def first_body(ws, mine, other, ee, qq, out):
    step = 64
    for half, qg in ((0, mine), (1, other)):

        @pl.loop(0, ROWS // step)
        def _(i):
            r = pl.multiple_of(i * step, step)
            at = pl.multiple_of(half * ROWS + r, step)
            rows = pl.ds(at, step)
            below = pl.ds(pl.multiple_of(at + 2 * ROWS, step), step)
            wv = ws[rows, 0:1]
            dv = ws[rows, 1:2]
            q = qg[pl.ds(r, step), C : C + W].astype(F32)
            g = qg[pl.ds(r, step), :C].astype(F32)
            qs = q * (SCALE * wv)
            qq[rows, :] = qs.astype(BF)
            qd = qs * dv
            qq[below, :C] = (g * wv - qd[:, :C]).astype(BF)
            qq[below, C:] = (-qd[:, C:]).astype(BF)

    key_parts(qq, ee, out)


def parts_body(qq, ee, out):
    key_parts(qq, ee, out)


def query_body(st, their, kt, e0, e1, mine, other, ws):
    row_factors(st, their, ws)
    for half, out in ((0, mine), (1, other)):
        xs = []
        for top in (0, 2 * ROWS):
            rows = slice(top + half * ROWS, top + (half + 1) * ROWS)
            acc = None
            at = 0
            for e in (e0, e1):
                n = e.shape[1]
                r = dot(e[rows, :], kt[:, at : at + n], 1, 1)
                acc = r if acc is None else acc + r
                at += n
            xs.append(acc)
        rows = slice(half * ROWS, (half + 1) * ROWS)
        w = ws[rows, 0:1]
        shift = ws[rows, 1:2]
        out[:, :C] = (w * xs[1][:, :C]).astype(out.dtype)
        out[:, C : C + W] = ((SCALE * w) * (xs[0] - shift * xs[1])).astype(out.dtype)
        out[:, C + W :] = jnp.zeros((ROWS, DR), out.dtype)


def tail_body(scal, qo, both, w, gq, keep, send, terms):
    for h in range(HEADS):
        rows = slice(h * NQ, (h + 1) * NQ)
        o = qo[rows, :C]
        lat = qo[rows, C : 2 * C]
        nope = both[:, h * (DN + DR) : h * (DN + DR) + DN]
        at = HEADS * (DN + DR) + h * DV
        grad = both[:, at : at + DV]
        c0 = h * (DN + DV)
        terms[:, c0 : c0 + DN] = dot(lat, nope, 0, 0).astype(BF)
        terms[:, c0 + DN : c0 + DN + DV] = dot(o, grad, 0, 0).astype(BF)
        q0 = h * (DN + DR)
        gq[:, q0 : q0 + DN] = dot(lat, w[:, c0 : c0 + DN]).astype(BF)
        gq[:, q0 + DN : q0 + DN + DR] = qo[rows, 2 * C : C + W]
    x, c = scal[2], scal[3]
    n = C // 8
    for k in range(4):
        base = lax.rem(x + k, 4) * (2 * n)
        slot = slice(k * n, (k + 1) * n)
        keep[slot, :] = terms[pl.ds(pl.multiple_of(base + c * n, n), n), :]
        send[slot, :] = terms[pl.ds(pl.multiple_of(base + (1 - c) * n, n), n), :]


def plus(a, b):
    return (a.astype(F32) + b.astype(F32)).astype(BF)


def step(queries, grad_out, latent, latent_up, query_start, key_lengths):
    ndev = NZ * NY
    own_q = queries.shape[1]

    own = latent[0].T
    both = jnp.concatenate(
        [
            queries.reshape(own_q, ndev, HEADS * (DN + DR)),
            grad_out.reshape(own_q, ndev, HEADS * DV),
        ],
        axis=2,
    )
    both = jnp.moveaxis(both, 1, 0)
    both = lax.all_to_all(both, CTX, 0, 0, tiled=True)
    both = both.reshape(NQ, HEADS * (DN + DR + DV))

    near = {0: homeward(own, 0)}
    near[-1], near[1] = homeward(own, 1), homeward(own, -1)
    for j in (2, 3):
        near[-j] = along_z(near[1 - j], 1)
        near[j] = along_z(near[j - 1], -1)
    near[4] = along_z(near[-3], 1)
    kept = [near[d] for d in OFFSETS]

    (qg,) = call(
        latents_body,
        [vmem((ROWS, WIDE), BF)],
        (query_start, key_lengths, both, in_hbm(latent_up)),
        270_000_000,
        smem=2,
        mib=12,
    )
    qg_mine = turn(qg, 0)
    qg_other = turn(qg, 1)
    (mine_side,) = call(join_body, [vmem((W, NZ * BLK), BF)], kept, 1_000_000, mib=6)
    their_side = other_core(mine_side)

    zi = lax.axis_index("z")
    yi = lax.axis_index("y")
    ci = lax.axis_index("core")
    y_own = jnp.where((yi >> 1) == ci, yi, 3 - yi)
    scal = jnp.stack([zi, y_own, lax.axis_index("x"), ci]).astype(jnp.int32)
    half = vmem((4 * ROWS, NZ * BLK), BF)
    big = pltpu.VMEM((2 * ROWS, KEYS), F32)
    e_mine, e_their, kt, stats = call(
        scores_body,
        [half, half, vmem((W, KEYS), BF), vmem((8, 2 * ROWS), F32)],
        (scal, qg_mine, qg_other, mine_side, their_side),
        2_280_000_000,
        (big, big, pltpu.VMEM((2 * ROWS, BLK), F32)),
        smem=1,
    )
    theirs = pair_y(stats)

    mine, other, ws = call(
        query_body,
        [vmem((ROWS, WIDE), BF), vmem((ROWS, WIDE), BF), vmem((2 * ROWS, BLK), F32)],
        (stats, theirs, kt, e_mine, e_their),
        2_400_000_000,
    )
    mine, other = turn(mine, 0), turn(other, 1)
    piece = vmem((NZ, W, BLK), BF)
    qq, their_keys = call(
        first_body,
        [vmem((4 * ROWS, W), BF), piece],
        (ws, qg_mine, qg_other, e_their),
        1_300_000_000,
    )
    their_keys = other_core(their_keys)
    (mine_keys,) = call(parts_body, [piece], (qq, e_mine), 1_200_000_000)
    sums = call(add_body, [vmem((W, BLK), BF)] * NZ, (mine_keys, their_keys), 1_000_000, mib=8)
    part = dict(zip(OFFSETS, sums))
    f = along_z(part[4], 1)
    b = along_z(part[-3], -1)
    stay = homeward(part[0], 0)
    f = plus(part[3], f)
    b = plus(part[-2], b)
    f = along_z(f, 1)
    b = along_z(b, -1)
    f = plus(part[2], f)
    b = plus(part[-1], b)
    f = along_z(f, 1)
    b = homeward(b, -1)
    f = plus(part[1], f)
    f = homeward(f, 1)
    key_grad = (stay.astype(F32) + b.astype(F32) + f.astype(F32)).T

    qo = (mine.astype(F32) + other.astype(F32)).astype(BF)
    wide = HEADS * (DN + DV)
    gq, keep, send = call(
        tail_body,
        [vmem((NQ, HEADS * (DN + DR)), BF)] + [vmem((C // 2, wide), BF)] * 2,
        (scal, qo, both, latent_up),
        200_000_000,
        (pltpu.VMEM((C, wide), BF),),
        smem=1,
        mib=12,
    )
    got = other_core(send)
    n = C // 8
    grad_weights = keep[:n].astype(F32) + got[:n].astype(F32)
    for k in range(1, 4):
        rows = slice(k * n, (k + 1) * n)
        pair = (keep[rows].astype(F32) + got[rows].astype(F32)).astype(BF)
        pair = lax.ppermute(pair, "x", [(i, (i + k) % 4) for i in range(4)])
        grad_weights = grad_weights + pair.astype(F32)
    back = lax.all_to_all(gq.reshape(ndev, own_q, HEADS * (DN + DR)), CTX, 0, 0, tiled=True)
    grad_queries = jnp.moveaxis(back, 0, 1).reshape(1, own_q, -1).astype(F32)
    return (grad_queries, key_grad[None], grad_weights)


def solution(mesh):
    finer = Mesh(mesh.devices.reshape(4, 2, NZ, NY), ("x", "core", "z", "y"))
    in_specs = (
        P(DP, CTX, None),
        P(DP, CTX, None),
        P(DP, CTX, None),
        P(None, CTX),
        P(DP),
        P(DP),
    )
    out_specs = (P(DP, CTX, None), P(DP, CTX, None), P(DP, CTX))
    return jax.shard_map(step, mesh=finer, in_specs=in_specs, out_specs=out_specs, check_vma=False)
```

```python
import math

import jax
import jax.numpy as jnp
from jax import lax
from jax.experimental import pallas as pl
from jax.experimental.pallas import tpu as pltpu
from jax.sharding import Mesh
from jax.sharding import PartitionSpec as P


DN = 128
DR = 64
DV = 128
C = 512
W = C + DR
NZ = 8
NY = 4
HEADS = 4
NQ = 64
ROWS = NQ * HEADS
WIDE = 2 * C + 2 * DR
BLK = 128
DP = ("x", "core")
CTX = ("z", "y")
MSCALE = 0.1 * math.log(40.0) + 1.0
SCALE = MSCALE * MSCALE / math.sqrt(DN + DR)
NEG_FILL = -1e30
BF = jnp.bfloat16
F32 = jnp.float32
OFFSETS = (0, 4, -3, 3, -2, 2, -1, 1)
KEYS = 2 * NZ * BLK
TILE = 256


def turned(flip):
    pairs = []
    for c in range(2):
        for y in range(NY):
            v, w = y >> 1, y & 1
            pairs.append((c * NY + y, v * NY + 2 * c + (w ^ flip)))
    return pairs


def turn(v, flip):
    return lax.ppermute(v, ("core", "y"), turned(flip))


def homeward(v, d):
    pairs = []
    for c in range(2):
        for z in range(NZ):
            for y in range(NY):
                here = (y >> 1) == c
                to = (c, y) if here else (1 - c, 3 - y)
                pairs.append(((c * NZ + z) * NY + y, (to[0] * NZ + (z + d) % NZ) * NY + to[1]))
    return lax.ppermute(v, ("core", "z", "y"), pairs)


def other_core(v):
    return lax.ppermute(v, "core", [(0, 1), (1, 0)])


def pair_y(v):
    return lax.ppermute(v, "y", [(i, i ^ 1) for i in range(NY)])


def along_z(v, step):
    return lax.ppermute(v, "z", [(i, (i + step) % NZ) for i in range(NZ)])


def dot(a, b, da=1, db=0):
    return lax.dot_general(a, b, (((da,), (db,)), ((), ())), preferred_element_type=F32)


def in_hbm(v):
    return pltpu.with_memory_space_constraint(v, pltpu.HBM)


def vmem(shape, dtype):
    return jax.ShapeDtypeStruct(shape, dtype)


def call(body, out_shape, args, flops, scratch=(), smem=0, mib=32):
    specs = [pl.BlockSpec(memory_space=pltpu.SMEM)] * smem
    specs += [pl.BlockSpec(memory_space=pltpu.VMEM)] * (len(args) - smem)
    size = sum(a.size * a.dtype.itemsize for a in args)
    size += sum(o.size * o.dtype.itemsize for o in out_shape)
    return pl.pallas_call(
        body,
        out_shape=out_shape,
        in_specs=specs,
        out_specs=[pl.BlockSpec(memory_space=pltpu.VMEM)] * len(out_shape),
        scratch_shapes=list(scratch),
        compiler_params=pltpu.CompilerParams(vmem_limit_bytes=mib * 1024 * 1024),
        cost_estimate=pl.CostEstimate(flops=flops, bytes_accessed=size, transcendentals=0),
    )(*args)


def latents_body(start, length, both, w, out):
    lane = lax.broadcasted_iota(jnp.int32, (NQ, DR), 1)
    note = jnp.zeros((NQ, DR), F32)
    low = start[0] + NQ - length[0]
    for n, v in enumerate((start[0] // NQ, start[0] % NQ, low // NQ, low % NQ)):
        note = jnp.where(lane == n, v.astype(F32), note)
    note = note.astype(BF)
    for h in range(HEADS):
        rows = slice(h * NQ, (h + 1) * NQ)
        nope = both[:, h * (DN + DR) : h * (DN + DR) + DN]
        rope = both[:, h * (DN + DR) + DN : (h + 1) * (DN + DR)]
        at = HEADS * (DN + DR) + h * DV
        grad = both[:, at : at + DV]
        wk = w[:, h * (DN + DV) : h * (DN + DV) + DN]
        wv = w[:, h * (DN + DV) + DN : (h + 1) * (DN + DV)]
        out[rows, :C] = dot(grad, wv, 1, 1).astype(BF)
        out[rows, C : 2 * C] = dot(nope, wk, 1, 1).astype(BF)
        out[rows, 2 * C : C + W] = rope
        out[rows, C + W :] = note


def join_body(*refs):
    for b in range(NZ):
        refs[NZ][:, b * BLK : (b + 1) * BLK] = refs[b][...]


def scores_body(*refs):
    scal, mine, other = refs[:3]
    keys = refs[3:5]
    e_mine, e_their, kt, stats, s_ref, gp_ref, wide = refs[5:]
    z, y_own = scal[0], scal[1]
    for n in range(2):
        kt[:, n * NZ * BLK : (n + 1) * NZ * BLK] = keys[n][...]
    note = mine[0:16, 2 * C :].astype(F32).astype(jnp.int32)[0:8, :]
    start = note[:, DR : DR + 1] * NQ + note[:, DR + 1 : DR + 2]
    low = note[:, DR + 2 : DR + 3] * NQ + note[:, DR + 3 : DR + 4]
    lane = lax.broadcasted_iota(jnp.int32, (8, BLK), 1)
    sub = lax.broadcasted_iota(jnp.int32, (8, BLK), 0)
    above = lane - low
    ahead = lane - start - sub
    base = []
    for y in (y_own, 3 - y_own):
        for d in OFFSETS:
            base.append(((z + d + NZ) % NZ) * (NY * BLK) + y * BLK)
    for half, qg in ((0, mine), (1, other)):
        rows = slice(half * ROWS, (half + 1) * ROWS)
        q = qg[:, C : C + W]
        g = qg[:, :C]
        for t in range(KEYS // TILE):
            cols = slice(t * TILE, (t + 1) * TILE)
            raw = dot(q, kt[:, cols])
            gp_ref[rows, cols] = dot(g, kt[:C, cols])
            inside = [above + base[2 * t + n] >= 0 for n in range(2)]
            gap = [ahead + base[2 * t + n] for n in range(2)]
            for j in range(NQ // 8):
                ok = [inside[n] & (gap[n] <= 8 * j) for n in range(2)]
                for h in range(HEADS):
                    r = slice(h * NQ + 8 * j, h * NQ + 8 * j + 8)
                    at = slice(half * ROWS + r.start, half * ROWS + r.stop)
                    v = [
                        jnp.where(ok[n], raw[r, n * BLK : (n + 1) * BLK], NEG_FILL)
                        for n in range(2)
                    ]
                    for n in range(2):
                        b = 2 * t + n
                        s_ref[at, b * BLK : (b + 1) * BLK] = v[n]
                    top = jnp.maximum(v[0], v[1])
                    wide[at, :] = top if t == 0 else jnp.maximum(wide[at, :], top)
    chunk = NQ

    @pl.loop(0, 2 * ROWS // chunk)
    def _(i):
        r0 = pl.multiple_of(i * chunk, chunk)
        here = pl.ds(r0, chunk)
        below = pl.ds(pl.multiple_of(2 * ROWS + r0, chunk), chunk)
        m = jnp.max(wide[here, :], axis=1, keepdims=True)
        safe = jnp.broadcast_to(jnp.maximum(m, 0.1 * NEG_FILL), (chunk, BLK))
        total = None
        rsum = None
        for b in range(16):
            cols = slice(b * BLK, (b + 1) * BLK)
            e = jnp.exp2((s_ref[here, cols] - safe) * (SCALE * math.log2(math.e)))
            s_ref[here, cols] = e
            p = e * gp_ref[here, cols]
            total = e if total is None else total + e
            rsum = p if rsum is None else rsum + p
        l = jnp.sum(total, axis=1, keepdims=True)
        rd = jnp.sum(rsum, axis=1, keepdims=True) / jnp.where(l > 0.0, l, 1.0)
        rdb = jnp.broadcast_to(rd, (chunk, BLK))
        for b in range(16):
            cols = slice(b * BLK, (b + 1) * BLK)
            out = e_mine if b < 8 else e_their
            oc = slice((b % 8) * BLK, (b % 8 + 1) * BLK)
            e = s_ref[here, cols]
            out[here, oc] = (e * (gp_ref[here, cols] - rdb)).astype(BF)
            out[below, oc] = e.astype(BF)
        col = lax.broadcasted_iota(jnp.int32, (chunk, BLK), 1)
        wide[here, :] = jnp.where(col == 0, m * SCALE, jnp.where(col == 1, l, rd))

    stats[...] = jnp.transpose(wide[...])[0:8, :]


def key_parts(qq, ee, out):
    for k in range(NZ // 2):
        r = dot(qq[...], ee[:, k * TILE : (k + 1) * TILE], 0, 0)
        for n in range(2):
            out[2 * k + n] = r[:, n * BLK : (n + 1) * BLK].astype(BF)


def add_body(a, b, *outs):
    for k in range(NZ):
        outs[k][...] = (a[k].astype(F32) + b[k].astype(F32)).astype(BF)


def row_factors(st, their, ws):
    there = jnp.concatenate([their[:, ROWS:], their[:, :ROWS]], axis=1)
    m, l, rd = st[0:1, :], st[1:2, :], st[2:3, :]
    m2, l2, rd2 = there[0:1, :], there[1:2, :], there[2:3, :]
    top = jnp.maximum(m, m2)
    a = jnp.exp(m - top)
    a2 = jnp.exp(m2 - top)
    denom = l * a + l2 * a2
    shift = (rd * l * a + rd2 * l2 * a2) / denom - rd
    row = lax.broadcasted_iota(jnp.int32, (BLK, 2 * ROWS), 0)
    ws[...] = jnp.transpose(jnp.where(row == 0, a / denom, shift))


def first_body(st, their, mine, other, ee, qq, out, ws):
    row_factors(st, their, ws)
    step = 64
    for half, qg in ((0, mine), (1, other)):

        @pl.loop(0, ROWS // step)
        def _(i):
            r = pl.multiple_of(i * step, step)
            at = pl.multiple_of(half * ROWS + r, step)
            rows = pl.ds(at, step)
            below = pl.ds(pl.multiple_of(at + 2 * ROWS, step), step)
            wv = ws[rows, 0:1]
            dv = ws[rows, 1:2]
            q = qg[pl.ds(r, step), C : C + W].astype(F32)
            g = qg[pl.ds(r, step), :C].astype(F32)
            qs = q * (SCALE * wv)
            qq[rows, :] = qs.astype(BF)
            qd = qs * dv
            qq[below, :C] = (g * wv - qd[:, :C]).astype(BF)
            qq[below, C:] = (-qd[:, C:]).astype(BF)

    key_parts(qq, ee, out)


def parts_body(qq, ee, out):
    key_parts(qq, ee, out)


def query_body(ws, kt, e0, e1, mine, other):
    for half, out in ((0, mine), (1, other)):
        xs = []
        for top in (0, 2 * ROWS):
            rows = slice(top + half * ROWS, top + (half + 1) * ROWS)
            acc = None
            at = 0
            for e in (e0, e1):
                n = e.shape[1]
                r = dot(e[rows, :], kt[:, at : at + n], 1, 1)
                acc = r if acc is None else acc + r
                at += n
            xs.append(acc)
        rows = slice(half * ROWS, (half + 1) * ROWS)
        w = ws[rows, 0:1]
        shift = ws[rows, 1:2]
        out[:, :C] = (w * xs[1][:, :C]).astype(out.dtype)
        out[:, C : C + W] = ((SCALE * w) * (xs[0] - shift * xs[1])).astype(out.dtype)
        out[:, C + W :] = jnp.zeros((ROWS, DR), out.dtype)


def tail_body(scal, qo, both, w, gq, keep, send, terms):
    for h in range(HEADS):
        rows = slice(h * NQ, (h + 1) * NQ)
        o = qo[rows, :C]
        lat = qo[rows, C : 2 * C]
        nope = both[:, h * (DN + DR) : h * (DN + DR) + DN]
        at = HEADS * (DN + DR) + h * DV
        grad = both[:, at : at + DV]
        c0 = h * (DN + DV)
        terms[:, c0 : c0 + DN] = dot(lat, nope, 0, 0).astype(BF)
        terms[:, c0 + DN : c0 + DN + DV] = dot(o, grad, 0, 0).astype(BF)
        q0 = h * (DN + DR)
        gq[:, q0 : q0 + DN] = dot(lat, w[:, c0 : c0 + DN]).astype(BF)
        gq[:, q0 + DN : q0 + DN + DR] = qo[rows, 2 * C : C + W]
    x, c = scal[2], scal[3]
    n = C // 8
    for k in range(4):
        base = lax.rem(x + k, 4) * (2 * n)
        slot = slice(k * n, (k + 1) * n)
        keep[slot, :] = terms[pl.ds(pl.multiple_of(base + c * n, n), n), :]
        send[slot, :] = terms[pl.ds(pl.multiple_of(base + (1 - c) * n, n), n), :]


def plus(a, b):
    return (a.astype(F32) + b.astype(F32)).astype(BF)


def step(queries, grad_out, latent, latent_up, query_start, key_lengths):
    ndev = NZ * NY
    own_q = queries.shape[1]

    own = latent[0].T
    both = jnp.concatenate(
        [
            queries.reshape(own_q, ndev, HEADS * (DN + DR)),
            grad_out.reshape(own_q, ndev, HEADS * DV),
        ],
        axis=2,
    )
    both = jnp.moveaxis(both, 1, 0)
    both = lax.all_to_all(both, CTX, 0, 0, tiled=True)
    both = both.reshape(NQ, HEADS * (DN + DR + DV))

    near = {0: homeward(own, 0)}
    near[-1], near[1] = homeward(own, 1), homeward(own, -1)
    for j in (2, 3):
        near[-j] = along_z(near[1 - j], 1)
        near[j] = along_z(near[j - 1], -1)
    near[4] = along_z(near[-3], 1)
    kept = [near[d] for d in OFFSETS]

    (qg,) = call(
        latents_body,
        [vmem((ROWS, WIDE), BF)],
        (query_start, key_lengths, both, in_hbm(latent_up)),
        270_000_000,
        smem=2,
        mib=12,
    )
    qg_mine = turn(qg, 0)
    qg_other = turn(qg, 1)
    (mine_side,) = call(join_body, [vmem((W, NZ * BLK), BF)], kept, 1_000_000, mib=6)
    their_side = other_core(mine_side)

    zi = lax.axis_index("z")
    yi = lax.axis_index("y")
    ci = lax.axis_index("core")
    y_own = jnp.where((yi >> 1) == ci, yi, 3 - yi)
    scal = jnp.stack([zi, y_own, lax.axis_index("x"), ci]).astype(jnp.int32)
    half = vmem((4 * ROWS, NZ * BLK), BF)
    big = pltpu.VMEM((2 * ROWS, KEYS), F32)
    e_mine, e_their, kt, stats = call(
        scores_body,
        [half, half, vmem((W, KEYS), BF), vmem((8, 2 * ROWS), F32)],
        (scal, qg_mine, qg_other, mine_side, their_side),
        2_280_000_000,
        (big, big, pltpu.VMEM((2 * ROWS, BLK), F32)),
        smem=1,
    )
    theirs = pair_y(stats)

    piece = vmem((NZ, W, BLK), BF)
    qq, their_keys, ws = call(
        first_body,
        [vmem((4 * ROWS, W), BF), piece, vmem((2 * ROWS, BLK), F32)],
        (stats, theirs, qg_mine, qg_other, e_their),
        1_300_000_000,
    )
    their_keys = other_core(their_keys)
    mine, other = call(
        query_body,
        [vmem((ROWS, WIDE), BF), vmem((ROWS, WIDE), BF)],
        (ws, kt, e_mine, e_their),
        2_400_000_000,
    )
    mine, other = turn(mine, 0), turn(other, 1)
    (mine_keys,) = call(parts_body, [piece], (qq, e_mine), 1_200_000_000)
    sums = call(add_body, [vmem((W, BLK), BF)] * NZ, (mine_keys, their_keys), 1_000_000, mib=8)
    part = dict(zip(OFFSETS, sums))
    f = along_z(part[4], 1)
    b = along_z(part[-3], -1)
    stay = homeward(part[0], 0)
    f = plus(part[3], f)
    b = plus(part[-2], b)
    f = along_z(f, 1)
    b = along_z(b, -1)
    f = plus(part[2], f)
    b = plus(part[-1], b)
    f = along_z(f, 1)
    b = homeward(b, -1)
    f = plus(part[1], f)
    f = homeward(f, 1)
    key_grad = (stay.astype(F32) + b.astype(F32) + f.astype(F32)).T

    qo = (mine.astype(F32) + other.astype(F32)).astype(BF)
    wide = HEADS * (DN + DV)
    gq, keep, send = call(
        tail_body,
        [vmem((NQ, HEADS * (DN + DR)), BF)] + [vmem((C // 2, wide), BF)] * 2,
        (scal, qo, both, latent_up),
        200_000_000,
        (pltpu.VMEM((C, wide), BF),),
        smem=1,
        mib=12,
    )
    got = other_core(send)
    n = C // 8
    grad_weights = keep[:n].astype(F32) + got[:n].astype(F32)
    for k in range(1, 4):
        rows = slice(k * n, (k + 1) * n)
        pair = (keep[rows].astype(F32) + got[rows].astype(F32)).astype(BF)
        pair = lax.ppermute(pair, "x", [(i, (i + k) % 4) for i in range(4)])
        grad_weights = grad_weights + pair.astype(F32)
    back = lax.all_to_all(gq.reshape(ndev, own_q, HEADS * (DN + DR)), CTX, 0, 0, tiled=True)
    grad_queries = jnp.moveaxis(back, 0, 1).reshape(1, own_q, -1).astype(F32)
    return (grad_queries, key_grad[None], grad_weights)


def solution(mesh):
    finer = Mesh(mesh.devices.reshape(4, 2, NZ, NY), ("x", "core", "z", "y"))
    in_specs = (
        P(DP, CTX, None),
        P(DP, CTX, None),
        P(DP, CTX, None),
        P(None, CTX),
        P(DP),
        P(DP),
    )
    out_specs = (P(DP, CTX, None), P(DP, CTX, None), P(DP, CTX))
    return jax.shard_map(step, mesh=finer, in_specs=in_specs, out_specs=out_specs, check_vma=False)
```

```python
import math

import jax
import jax.numpy as jnp
from jax import lax
from jax.experimental import pallas as pl
from jax.experimental.pallas import tpu as pltpu
from jax.sharding import Mesh
from jax.sharding import PartitionSpec as P


DN = 128
DR = 64
DV = 128
C = 512
W = C + DR
NZ = 8
NY = 4
HEADS = 4
NQ = 64
ROWS = NQ * HEADS
WIDE = 2 * C + 2 * DR
BLK = 128
DP = ("x", "core")
CTX = ("z", "y")
MSCALE = 0.1 * math.log(40.0) + 1.0
SCALE = MSCALE * MSCALE / math.sqrt(DN + DR)
NEG_FILL = -1e30
BF = jnp.bfloat16
F32 = jnp.float32
OFFSETS = (0, 4, -3, 3, -2, 2, -1, 1)
KEYS = 2 * NZ * BLK
TILE = 256


def turned(flip):
    pairs = []
    for c in range(2):
        for y in range(NY):
            v, w = y >> 1, y & 1
            pairs.append((c * NY + y, v * NY + 2 * c + (w ^ flip)))
    return pairs


def turn(v, flip):
    return lax.ppermute(v, ("core", "y"), turned(flip))


def homeward(v, d):
    pairs = []
    for c in range(2):
        for z in range(NZ):
            for y in range(NY):
                here = (y >> 1) == c
                to = (c, y) if here else (1 - c, 3 - y)
                pairs.append(((c * NZ + z) * NY + y, (to[0] * NZ + (z + d) % NZ) * NY + to[1]))
    return lax.ppermute(v, ("core", "z", "y"), pairs)


def other_core(v):
    return lax.ppermute(v, "core", [(0, 1), (1, 0)])


def pair_y(v):
    return lax.ppermute(v, "y", [(i, i ^ 1) for i in range(NY)])


def along_z(v, step):
    return lax.ppermute(v, "z", [(i, (i + step) % NZ) for i in range(NZ)])


def dot(a, b, da=1, db=0):
    return lax.dot_general(a, b, (((da,), (db,)), ((), ())), preferred_element_type=F32)


def in_hbm(v):
    return pltpu.with_memory_space_constraint(v, pltpu.HBM)


def vmem(shape, dtype):
    return jax.ShapeDtypeStruct(shape, dtype)


def call(body, out_shape, args, flops, scratch=(), smem=0, mib=32):
    specs = [pl.BlockSpec(memory_space=pltpu.SMEM)] * smem
    specs += [pl.BlockSpec(memory_space=pltpu.VMEM)] * (len(args) - smem)
    size = sum(a.size * a.dtype.itemsize for a in args)
    size += sum(o.size * o.dtype.itemsize for o in out_shape)
    return pl.pallas_call(
        body,
        out_shape=out_shape,
        in_specs=specs,
        out_specs=[pl.BlockSpec(memory_space=pltpu.VMEM)] * len(out_shape),
        scratch_shapes=list(scratch),
        compiler_params=pltpu.CompilerParams(vmem_limit_bytes=mib * 1024 * 1024),
        cost_estimate=pl.CostEstimate(flops=flops, bytes_accessed=size, transcendentals=0),
    )(*args)


def latents_body(start, length, both, w, out):
    lane = lax.broadcasted_iota(jnp.int32, (NQ, DR), 1)
    note = jnp.zeros((NQ, DR), F32)
    low = start[0] + NQ - length[0]
    for n, v in enumerate((start[0] // NQ, start[0] % NQ, low // NQ, low % NQ)):
        note = jnp.where(lane == n, v.astype(F32), note)
    note = note.astype(BF)
    for h in range(HEADS):
        rows = slice(h * NQ, (h + 1) * NQ)
        nope = both[:, h * (DN + DR) : h * (DN + DR) + DN]
        rope = both[:, h * (DN + DR) + DN : (h + 1) * (DN + DR)]
        at = HEADS * (DN + DR) + h * DV
        grad = both[:, at : at + DV]
        wk = w[:, h * (DN + DV) : h * (DN + DV) + DN]
        wv = w[:, h * (DN + DV) + DN : (h + 1) * (DN + DV)]
        out[rows, :C] = dot(grad, wv, 1, 1).astype(BF)
        out[rows, C : 2 * C] = dot(nope, wk, 1, 1).astype(BF)
        out[rows, 2 * C : C + W] = rope
        out[rows, C + W :] = note


def join_body(*refs):
    for b in range(NZ):
        refs[NZ][:, b * BLK : (b + 1) * BLK] = refs[b][...]


def scores_body(*refs):
    scal, mine, other = refs[:3]
    keys = refs[3:5]
    e_mine, e_their, kt, stats, s_ref, gp_ref, wide = refs[5:]
    z, y_own = scal[0], scal[1]
    for n in range(2):
        kt[:, n * NZ * BLK : (n + 1) * NZ * BLK] = keys[n][...]
    note = mine[0:16, 2 * C :].astype(F32).astype(jnp.int32)[0:8, :]
    start = note[:, DR : DR + 1] * NQ + note[:, DR + 1 : DR + 2]
    low = note[:, DR + 2 : DR + 3] * NQ + note[:, DR + 3 : DR + 4]
    lane = lax.broadcasted_iota(jnp.int32, (8, BLK), 1)
    sub = lax.broadcasted_iota(jnp.int32, (8, BLK), 0)
    above = lane - low
    ahead = lane - start - sub
    base = []
    for y in (y_own, 3 - y_own):
        for d in OFFSETS:
            base.append(((z + d + NZ) % NZ) * (NY * BLK) + y * BLK)
    for half, qg in ((0, mine), (1, other)):
        rows = slice(half * ROWS, (half + 1) * ROWS)
        q = qg[:, C : C + W]
        g = qg[:, :C]
        for t in range(KEYS // TILE):
            cols = slice(t * TILE, (t + 1) * TILE)
            raw = dot(q, kt[:, cols])
            gp_ref[rows, cols] = dot(g, kt[:C, cols])
            inside = [above + base[2 * t + n] >= 0 for n in range(2)]
            gap = [ahead + base[2 * t + n] for n in range(2)]
            for j in range(NQ // 8):
                ok = [inside[n] & (gap[n] <= 8 * j) for n in range(2)]
                for h in range(HEADS):
                    r = slice(h * NQ + 8 * j, h * NQ + 8 * j + 8)
                    at = slice(half * ROWS + r.start, half * ROWS + r.stop)
                    v = [
                        jnp.where(ok[n], raw[r, n * BLK : (n + 1) * BLK], NEG_FILL)
                        for n in range(2)
                    ]
                    for n in range(2):
                        b = 2 * t + n
                        s_ref[at, b * BLK : (b + 1) * BLK] = v[n]
                    top = jnp.maximum(v[0], v[1])
                    wide[at, :] = top if t == 0 else jnp.maximum(wide[at, :], top)
    chunk = NQ

    @pl.loop(0, 2 * ROWS // chunk)
    def _(i):
        r0 = pl.multiple_of(i * chunk, chunk)
        here = pl.ds(r0, chunk)
        below = pl.ds(pl.multiple_of(2 * ROWS + r0, chunk), chunk)
        m = jnp.max(wide[here, :], axis=1, keepdims=True)
        safe = jnp.broadcast_to(jnp.maximum(m, 0.1 * NEG_FILL), (chunk, BLK))
        total = None
        rsum = None
        for b in range(16):
            cols = slice(b * BLK, (b + 1) * BLK)
            e = jnp.exp2((s_ref[here, cols] - safe) * (SCALE * math.log2(math.e)))
            s_ref[here, cols] = e
            p = e * gp_ref[here, cols]
            total = e if total is None else total + e
            rsum = p if rsum is None else rsum + p
        l = jnp.sum(total, axis=1, keepdims=True)
        rd = jnp.sum(rsum, axis=1, keepdims=True) / jnp.where(l > 0.0, l, 1.0)
        rdb = jnp.broadcast_to(rd, (chunk, BLK))
        for b in range(16):
            cols = slice(b * BLK, (b + 1) * BLK)
            out = e_mine if b < 8 else e_their
            oc = slice((b % 8) * BLK, (b % 8 + 1) * BLK)
            e = s_ref[here, cols]
            out[here, oc] = (e * (gp_ref[here, cols] - rdb)).astype(BF)
            out[below, oc] = e.astype(BF)
        col = lax.broadcasted_iota(jnp.int32, (chunk, BLK), 1)
        wide[here, :] = jnp.where(col == 0, m * SCALE, jnp.where(col == 1, l, rd))

    stats[...] = jnp.transpose(wide[...])[0:8, :]


def key_parts(qq, ee, out):
    for k in range(NZ // 2):
        r = dot(qq[...], ee[:, k * TILE : (k + 1) * TILE], 0, 0)
        for n in range(2):
            out[2 * k + n] = r[:, n * BLK : (n + 1) * BLK].astype(BF)


def add_body(a, b, *outs):
    for k in range(NZ):
        outs[k][...] = (a[k].astype(F32) + b[k].astype(F32)).astype(BF)


def row_factors(st, their, ws):
    there = jnp.concatenate([their[:, ROWS:], their[:, :ROWS]], axis=1)
    m, l, rd = st[0:1, :], st[1:2, :], st[2:3, :]
    m2, l2, rd2 = there[0:1, :], there[1:2, :], there[2:3, :]
    top = jnp.maximum(m, m2)
    a = jnp.exp(m - top)
    a2 = jnp.exp(m2 - top)
    denom = l * a + l2 * a2
    shift = (rd * l * a + rd2 * l2 * a2) / denom - rd
    row = lax.broadcasted_iota(jnp.int32, (BLK, 2 * ROWS), 0)
    ws[...] = jnp.transpose(jnp.where(row == 0, a / denom, shift))


def first_body(st, their, mine, other, ee, qq, out, ws):
    row_factors(st, their, ws)
    step = 64
    for half, qg in ((0, mine), (1, other)):

        @pl.loop(0, ROWS // step)
        def _(i):
            r = pl.multiple_of(i * step, step)
            at = pl.multiple_of(half * ROWS + r, step)
            rows = pl.ds(at, step)
            below = pl.ds(pl.multiple_of(at + 2 * ROWS, step), step)
            wv = ws[rows, 0:1]
            dv = ws[rows, 1:2]
            q = qg[pl.ds(r, step), C : C + W].astype(F32)
            g = qg[pl.ds(r, step), :C].astype(F32)
            qs = q * (SCALE * wv)
            qq[rows, :] = qs.astype(BF)
            qd = qs * dv
            qq[below, :C] = (g * wv - qd[:, :C]).astype(BF)
            qq[below, C:] = (-qd[:, C:]).astype(BF)

    key_parts(qq, ee, out)


def parts_body(qq, ee, out):
    key_parts(qq, ee, out)


def query_body(ws, kt, e0, e1, mine, other):
    for half, out in ((0, mine), (1, other)):
        xs = []
        for top in (0, 2 * ROWS):
            rows = slice(top + half * ROWS, top + (half + 1) * ROWS)
            acc = None
            at = 0
            for e in (e0, e1):
                n = e.shape[1]
                r = dot(e[rows, :], kt[:, at : at + n], 1, 1)
                acc = r if acc is None else acc + r
                at += n
            xs.append(acc)
        rows = slice(half * ROWS, (half + 1) * ROWS)
        w = ws[rows, 0:1]
        shift = ws[rows, 1:2]
        out[:, :C] = (w * xs[1][:, :C]).astype(out.dtype)
        out[:, C : C + W] = ((SCALE * w) * (xs[0] - shift * xs[1])).astype(out.dtype)
        out[:, C + W :] = jnp.zeros((ROWS, DR), out.dtype)


def tail_body(scal, qo, both, w, rows_out, keep, send, terms, gq):
    for h in range(HEADS):
        rows = slice(h * NQ, (h + 1) * NQ)
        o = qo[rows, :C]
        lat = qo[rows, C : 2 * C]
        nope = both[:, h * (DN + DR) : h * (DN + DR) + DN]
        at = HEADS * (DN + DR) + h * DV
        grad = both[:, at : at + DV]
        c0 = h * (DN + DV)
        terms[:, c0 : c0 + DN] = dot(lat, nope, 0, 0).astype(BF)
        terms[:, c0 + DN : c0 + DN + DV] = dot(o, grad, 0, 0).astype(BF)
        q0 = h * (DN + DR)
        gq[:, q0 : q0 + DN] = dot(lat, w[:, c0 : c0 + DN]).astype(BF)
        gq[:, q0 + DN : q0 + DN + DR] = qo[rows, 2 * C : C + W]
    for d in range(NZ * NY):
        rows_out[d] = gq[2 * d : 2 * d + 2, :]
    x, c = scal[2], scal[3]
    n = C // 8
    for k in range(4):
        base = lax.rem(x + k, 4) * (2 * n)
        slot = slice(k * n, (k + 1) * n)
        keep[slot, :] = terms[pl.ds(pl.multiple_of(base + c * n, n), n), :]
        send[slot, :] = terms[pl.ds(pl.multiple_of(base + (1 - c) * n, n), n), :]


def plus(a, b):
    return (a.astype(F32) + b.astype(F32)).astype(BF)


def step(queries, grad_out, latent, latent_up, query_start, key_lengths):
    ndev = NZ * NY
    own_q = queries.shape[1]

    own = latent[0].T
    both = jnp.concatenate(
        [
            queries.reshape(own_q, ndev, HEADS * (DN + DR)),
            grad_out.reshape(own_q, ndev, HEADS * DV),
        ],
        axis=2,
    )
    both = jnp.moveaxis(both, 1, 0)
    both = lax.all_to_all(both, CTX, 0, 0, tiled=True)
    both = both.reshape(NQ, HEADS * (DN + DR + DV))

    near = {0: homeward(own, 0)}
    near[-1], near[1] = homeward(own, 1), homeward(own, -1)
    for j in (2, 3):
        near[-j] = along_z(near[1 - j], 1)
        near[j] = along_z(near[j - 1], -1)
    near[4] = along_z(near[-3], 1)
    kept = [near[d] for d in OFFSETS]

    (qg,) = call(
        latents_body,
        [vmem((ROWS, WIDE), BF)],
        (query_start, key_lengths, both, in_hbm(latent_up)),
        270_000_000,
        smem=2,
        mib=12,
    )
    qg_mine = turn(qg, 0)
    qg_other = turn(qg, 1)
    (mine_side,) = call(join_body, [vmem((W, NZ * BLK), BF)], kept, 1_000_000, mib=6)
    their_side = other_core(mine_side)

    zi = lax.axis_index("z")
    yi = lax.axis_index("y")
    ci = lax.axis_index("core")
    y_own = jnp.where((yi >> 1) == ci, yi, 3 - yi)
    scal = jnp.stack([zi, y_own, lax.axis_index("x"), ci]).astype(jnp.int32)
    half = vmem((4 * ROWS, NZ * BLK), BF)
    big = pltpu.VMEM((2 * ROWS, KEYS), F32)
    e_mine, e_their, kt, stats = call(
        scores_body,
        [half, half, vmem((W, KEYS), BF), vmem((8, 2 * ROWS), F32)],
        (scal, qg_mine, qg_other, mine_side, their_side),
        2_280_000_000,
        (big, big, pltpu.VMEM((2 * ROWS, BLK), F32)),
        smem=1,
    )
    theirs = pair_y(stats)

    piece = vmem((NZ, W, BLK), BF)
    qq, their_keys, ws = call(
        first_body,
        [vmem((4 * ROWS, W), BF), piece, vmem((2 * ROWS, BLK), F32)],
        (stats, theirs, qg_mine, qg_other, e_their),
        1_300_000_000,
    )
    their_keys = other_core(their_keys)
    mine, other = call(
        query_body,
        [vmem((ROWS, WIDE), BF), vmem((ROWS, WIDE), BF)],
        (ws, kt, e_mine, e_their),
        2_400_000_000,
    )
    mine, other = turn(mine, 0), turn(other, 1)
    (mine_keys,) = call(parts_body, [piece], (qq, e_mine), 1_200_000_000)
    sums = call(add_body, [vmem((W, BLK), BF)] * NZ, (mine_keys, their_keys), 1_000_000, mib=8)
    part = dict(zip(OFFSETS, sums))
    f = along_z(part[4], 1)
    b = along_z(part[-3], -1)
    stay = homeward(part[0], 0)
    f = plus(part[3], f)
    b = plus(part[-2], b)
    f = along_z(f, 1)
    b = along_z(b, -1)
    f = plus(part[2], f)
    b = plus(part[-1], b)
    f = along_z(f, 1)
    b = homeward(b, -1)
    f = plus(part[1], f)
    f = homeward(f, 1)
    key_grad = (stay.astype(F32) + b.astype(F32) + f.astype(F32)).T

    qo = (mine.astype(F32) + other.astype(F32)).astype(BF)
    wide = HEADS * (DN + DV)
    gq, keep, send = call(
        tail_body,
        [vmem((ndev, own_q, HEADS * (DN + DR)), BF)] + [vmem((C // 2, wide), BF)] * 2,
        (scal, qo, both, latent_up),
        200_000_000,
        (pltpu.VMEM((C, wide), BF), pltpu.VMEM((NQ, HEADS * (DN + DR)), BF)),
        smem=1,
        mib=12,
    )
    got = other_core(send)
    n = C // 8
    grad_weights = keep[:n].astype(F32) + got[:n].astype(F32)
    for k in range(1, 4):
        rows = slice(k * n, (k + 1) * n)
        pair = (keep[rows].astype(F32) + got[rows].astype(F32)).astype(BF)
        pair = lax.ppermute(pair, "x", [(i, (i + k) % 4) for i in range(4)])
        grad_weights = grad_weights + pair.astype(F32)
    back = lax.all_to_all(gq, CTX, 0, 0, tiled=True)
    grad_queries = jnp.moveaxis(back, 0, 1).reshape(1, own_q, -1).astype(F32)
    return (grad_queries, key_grad[None], grad_weights)


def solution(mesh):
    finer = Mesh(mesh.devices.reshape(4, 2, NZ, NY), ("x", "core", "z", "y"))
    in_specs = (
        P(DP, CTX, None),
        P(DP, CTX, None),
        P(DP, CTX, None),
        P(None, CTX),
        P(DP),
        P(DP),
    )
    out_specs = (P(DP, CTX, None), P(DP, CTX, None), P(DP, CTX))
    return jax.shard_map(step, mesh=finer, in_specs=in_specs, out_specs=out_specs, check_vma=False)
```
